128 devices in a mesh: prod: 8 (over y_hi, x), cand: 16 (over y_lo, z, core).
Axes of the slice: x: 4, y: 4 (y_hi: 2, y_lo: 2; y = y_hi * 2 + y_lo), z: 4, core: 2. Of those that a mesh axis runs over, the one named last changes fastest.
Arguments:
- cand_states: bfloat16 [8, 16, 128, 4096], P('prod', 'cand'), may hold values from -600 to 600
- enc_rows: bfloat16 [8, 256, 4096], P('prod', 'cand'), may hold values from -120 to 120
- w_query: bfloat16 [4096, 4096], P('prod', 'cand'), may hold values from -0.09375 to 0.09375
- w_key: bfloat16 [4096, 4096], P('prod', 'cand'), may hold values from -0.09375 to 0.09375
- w_value: bfloat16 [4096, 4096], P('prod', 'cand'), may hold values from -0.09375 to 0.09375
- w_out: bfloat16 [4096, 4096], P('cand', 'prod'), may hold values from -0.375 to 0.375
- tile_mask: int32 [8, 16, 2], P('prod', 'cand'), may hold values from 0 to 1, as said below
- counts: int32 [8], P('prod'), may hold values from 1 to 16, as said below
Outputs:
- cross_out: bfloat16 [8, 16, 128, 4096], P('prod', 'cand')
The draws below stay inside these ranges and needn't reach their ends.
Inputs may be any that keep to these rules, and one draw needn't show every extreme that they name: `tile_mask`: every candidate has at least one tile set. `counts`: some product fills all 16 slots.
All inputs are finite; a program needn't handle non-finite values.
Results may differ from the reference program's by a relative error of at most 0.023.
The reference program's roundings to bfloat16 on the way count: a program that leaves them out, or rounds other values in their place, can miss the bound.
Values may be sent and summed in bfloat16 or wider, within the bound.
A program may use at most 128 MiB of HBM per device.

```python
import math
import jax
import jax.numpy as jnp
from jax import lax

D = 4096
HEADS = 64
HD = 64
CLEN = 128
ELEN = 256
TILE = 128
ETILES = 2
PRODUCTS = 8
CANDS = 16
GROUP = 256
N_CAND = 16


def draw_cand_states(key, part):
    first, second, third = jax.random.split(key, 3)
    shape = (PRODUCTS, CANDS, CLEN, D)
    row_scale = jnp.exp(jax.random.uniform(first, (PRODUCTS, CANDS, CLEN, 1), jnp.float32, 0.0, math.log(10.0)))
    col_scale = jnp.exp(jax.random.uniform(second, (D,), jnp.float32, 0.0, math.log(10.0)))
    base = jnp.clip(jax.random.normal(third, shape, jnp.float32), -4.0, 4.0)
    return (base * row_scale * col_scale).astype(jnp.bfloat16)


def draw_enc_rows(key, part):
    first = jax.random.fold_in(key, 0)
    shape = (PRODUCTS, ELEN, D)
    base = jnp.clip(jax.random.normal(first, shape, jnp.float32), -4.0, 4.0)
    return base.astype(jnp.bfloat16)


def draw_tile_mask(key, part):
    first, second = jax.random.split(key, 2)
    bits = jax.random.randint(first, (PRODUCTS, CANDS, ETILES), 0, 2)
    forced = jax.random.randint(second, (PRODUCTS, CANDS, 1), 0, ETILES)
    places = jnp.arange(ETILES).astype(jnp.int32)[None, None, :]
    return jnp.maximum(bits, (places == forced).astype(jnp.int32)).astype(jnp.int32)


def draw_counts(key, part):
    first, second = jax.random.split(key, 2)
    filled = jax.random.randint(first, (PRODUCTS,), 1, CANDS + 1)
    chosen = jax.random.randint(second, (), 0, PRODUCTS)
    places = jnp.arange(PRODUCTS).astype(jnp.int32)
    return jnp.where(places == chosen, CANDS, filled).astype(jnp.int32)


def block_scale(rng, dims, cuts, least, top_value):
    gain, own = 1.0, jax.random.fold_in(rng, 6)
    for position, shards_of in cuts:
        steps = jnp.exp(jax.random.uniform(jax.random.fold_in(own, position), (shards_of,), jnp.float32, least / len(cuts), top_value / len(cuts)))
        gain = gain * jnp.repeat(steps, dims[position] // shards_of).reshape([-1 if axis == position else 1 for axis in range(len(dims))])
    return gain


def noise(key, dims, width, limit, cuts=(), held_as=jnp.bfloat16):
    drawn = width * jax.random.normal(key, dims, jnp.float32)
    if cuts:
        drawn = drawn * block_scale(key, dims, cuts, -0.22, 0.18)
    return jnp.clip(drawn, -limit, limit).astype(held_as)


def setup_inputs(seed: int = 0) -> dict:
    arg_keys = jax.random.split(jax.random.key(seed), 9)
    cand_states = draw_cand_states(jax.random.fold_in(arg_keys[8], 71), 0)
    enc_rows = draw_enc_rows(jax.random.fold_in(arg_keys[8], 71), 0)
    w_query = noise(arg_keys[2], (D, D), D ** -0.5, 0.09375, ((0, 8), (1, 16)))
    w_key = noise(arg_keys[3], (D, D), D ** -0.5, 0.09375, ((0, 8), (1, 16)))
    w_value = noise(arg_keys[4], (D, D), D ** -0.5, 0.09375, ((0, 8), (1, 16)))
    w_out = noise(arg_keys[5], (D, D), (HD * 4) ** -0.5, 0.375, ((0, 16), (1, 8)))
    tile_mask = draw_tile_mask(jax.random.fold_in(arg_keys[8], 71), 0)
    counts = draw_counts(jax.random.fold_in(arg_keys[8], 71), 0)
    return dict(cand_states=cand_states, enc_rows=enc_rows, w_query=w_query, w_key=w_key, w_value=w_value, w_out=w_out, tile_mask=tile_mask, counts=counts)


def normalize(rows):
    values = rows.astype(jnp.float32)
    scale = lax.rsqrt(lax.optimization_barrier(jnp.mean(values * values, axis=-1, keepdims=True)) + 1e-06)
    return (values * scale).astype(jnp.bfloat16)

def reference(cand_states, enc_rows, w_query, w_key, w_value, w_out, tile_mask, counts):
    key_tile = (jnp.arange(ELEN) // TILE).astype(jnp.int32)

    def one_product(items):
        states, encoder, flags, count = items
        normed = normalize(states).reshape(CANDS * CLEN, D)
        query = jnp.dot(normed, w_query, preferred_element_type=jnp.float32).astype(jnp.bfloat16)
        keys = jnp.dot(encoder, w_key, preferred_element_type=jnp.float32).astype(jnp.bfloat16)
        values = jnp.dot(encoder, w_value, preferred_element_type=jnp.float32).astype(jnp.bfloat16)
        query = query.reshape(CANDS, CLEN, HEADS, HD).astype(jnp.float32)
        keys = keys.reshape(ELEN, HEADS, HD).astype(jnp.float32)
        values = values.reshape(ELEN, HEADS, HD).astype(jnp.float32)
        scores = jnp.einsum('clhd,ehd->chle', query, keys) * 0.125
        open_keys = flags[:, key_tile] > 0
        scores = jnp.where(open_keys[:, None, None, :], scores, -1e+30)
        top = lax.optimization_barrier(jnp.max(scores, axis=-1, keepdims=True))
        weights = jnp.exp(scores - top)
        probs = (weights / lax.optimization_barrier(jnp.sum(weights, axis=-1, keepdims=True))).astype(jnp.bfloat16)
        context = jnp.einsum('chle,ehd->clhd', probs.astype(jnp.float32), values).astype(jnp.bfloat16)
        context = context.reshape(CANDS * CLEN, D)

        def add_group(index, total):
            start = (index * GROUP).astype(jnp.int32)
            left = lax.dynamic_slice_in_dim(context, start, GROUP, 1)
            right = lax.dynamic_slice_in_dim(w_out, start, GROUP, 0)
            term = lax.optimization_barrier(jnp.dot(left, right, preferred_element_type=jnp.float32).astype(jnp.bfloat16))
            return total + term.astype(jnp.float32)
        total = lax.fori_loop(0, N_CAND, add_group, jnp.zeros((CANDS * CLEN, D), jnp.float32))
        live = (jnp.arange(CANDS).astype(jnp.int32) < count).astype(jnp.float32)
        return (total.reshape(CANDS, CLEN, D) * live[:, None, None]).astype(jnp.bfloat16)
    return lax.map(one_product, (cand_states, enc_rows, tile_mask, counts))
```

```python
import functools

import jax
import jax.numpy as jnp
from jax import lax
from jax.experimental import pallas as pl
from jax.experimental.pallas import tpu as pltpu
from jax.sharding import PartitionSpec as P

MESH = pl.DeviceIdType.MESH
F32, BF16 = jnp.float32, jnp.bfloat16
MAX_COPIES = 192


def kernel(
    x_ref, enc_ref, wq_ref, wk_ref, wv_ref, wo_ref, mask_ref, out_ref,
    xbuf, rows, masks, enc, wq, wk, wv, wo, kv, kmask, vmask, query, ctx,
    part, tsend, trecv, fsend, frecv, send_sem, recv_sem, local_sem,
):
    p, c = lax.axis_index("prod"), lax.axis_index("cand")
    yh, x = p // 4, lax.rem(p, 4)
    yl, z, k = c // 8, lax.rem(c // 2, 4), lax.rem(c, 2)
    y = yh * 2 + yl
    step = lambda v, d: lax.rem(v + (d + 4), 4)

    def dev(yy, xx, zz, kk):
        return (yy // 2) * 4 + xx, lax.rem(yy, 2) * 8 + zz * 2 + kk

    sib = dev(y, x, z, 1 - k)
    xup, xdn = dev(y, step(x, 1), z, k), dev(y, step(x, -1), z, k)
    yup, ydn = dev(step(y, 1), x, z, k), dev(step(y, -1), x, z, k)
    yfar = dev(step(y, 2), x, z, k)
    ypair = dev(yh * 2 + 1 - yl, x, z, k)
    zup, zdn = dev(y, x, step(z, 1), k), dev(y, x, step(z, -1), k)

    barrier = pltpu.get_barrier_semaphore()
    peers = (sib, xup, xdn, yup, ydn, yfar, zup, zdn)
    for d in peers:
        pl.semaphore_signal(barrier, inc=1, device_id=d, device_id_type=MESH)

    count = [0]
    sends = []

    def send(src, there, here, d):
        i = count[0]
        count[0] += 1
        go = pltpu.make_async_remote_copy(
            src_ref=src, dst_ref=there, send_sem=send_sem.at[i], recv_sem=recv_sem.at[i],
            device_id=d, device_id_type=MESH,
        )
        go.start()
        sends.append(go)
        return pltpu.make_async_remote_copy(
            src_ref=src, dst_ref=here, send_sem=send_sem.at[i], recv_sem=recv_sem.at[i],
            device_id=d, device_id_type=MESH,
        ).wait_recv

    nlocal = [0]

    def local(src, dst):
        i = nlocal[0]
        nlocal[0] += 1
        copy = pltpu.make_async_copy(src, dst, local_sem.at[i])
        copy.start()
        return copy.wait

    load_x = local(x_ref, xbuf)
    loads = [
        local(wk_ref, wk.at[p]), local(wv_ref, wv.at[p]), local(enc_ref, enc.at[c]),
        local(mask_ref, masks.at[z]),
        local(wq_ref, wq.at[p, yl * 2 + k]), local(wo_ref, wo.at[p, yl * 2 + k]),
    ]
    pl.semaphore_wait(barrier, len(peers))

    class Plane:
        def __init__(self, src, buf, half):
            self.src, self.buf, self.half = src, buf, half
            self.order = (x, step(x, -1), step(x, 1), step(x, 2))
            self.got_y, self.got_far, self.got_sib = {}, {}, {i: [] for i in range(4)}

        def slot(self, yy, xx, kk):
            return self.buf.at[(yy // 2) * 4 + xx, lax.rem(yy, 2) * 2 + kk]

        def first(self, yy, xx):
            return self.slot(yy, xx, k).at[pl.ds(0, self.half)]

        def second(self, yy, xx):
            return self.slot(yy, xx, k).at[pl.ds(self.half, self.half)]

        def x_start(self):
            here = self.slot(y, x, k)
            self.got_x = [
                send(self.src, here, self.slot(y, step(x, -1), k), xup),
                send(self.src, here, self.slot(y, step(x, 1), k), xdn),
            ]

        def x_forward(self):
            for got in self.got_x:
                got()
            far = step(x, 2)
            lo, hi = step(x, -1), step(x, 1)
            self.got_xfar = [
                send(self.first(y, lo), self.first(y, lo), self.first(y, far), xup),
                send(self.second(y, hi), self.second(y, hi), self.second(y, far), xdn),
            ]

        def x_finish(self):
            for got in self.got_xfar:
                got()

        def cross(self, i, yy):
            xx = self.order[i]
            here = self.slot(yy, xx, k)
            src = self.src if i == 0 and yy is y else here
            self.got_sib[i].append(send(src, here, self.slot(yy, xx, 1 - k), sib))

        def y_start(self, i):
            xx = self.order[i]
            here = self.slot(y, xx, k)
            src = self.src if i == 0 else here
            self.got_y[i] = [
                send(src, here, self.slot(step(y, -1), xx, k), yup),
                send(src, here, self.slot(step(y, 1), xx, k), ydn),
            ]
            self.cross(i, y)

        def y_forward(self, i):
            xx = self.order[i]
            for got in self.got_y[i]:
                got()
            lo, hi, far = step(y, -1), step(y, 1), step(y, 2)
            self.got_far[i] = [
                send(self.first(lo, xx), self.first(lo, xx), self.first(far, xx), yup),
                send(self.second(hi, xx), self.second(hi, xx), self.second(far, xx), ydn),
            ]
            self.cross(i, lo)
            self.cross(i, hi)

        def y_finish(self, i):
            for got in self.got_far[i]:
                got()
            self.cross(i, step(y, 2))

        def ready(self, i):
            for got in self.got_sib[i]:
                got()

    def kv_ring(src, buf, g):
        here = buf.at[g * 4 + x]
        return [
            send(src, here, buf.at[g * 4 + step(x, -1)], xup),
            send(src, here, buf.at[g * 4 + step(x, 1)], xdn),
        ]

    def kv_forward(buf, g):
        lo, hi, far = (buf.at[g * 4 + step(x, d)] for d in (-1, 1, 2))
        a, b = pl.ds(0, 256), pl.ds(256, 256)
        return [
            send(lo.at[a], lo.at[a], far.at[a], xup),
            send(hi.at[b], hi.at[b], far.at[b], xdn),
        ]

    gq = Plane(wq_ref, wq, 256)
    go = Plane(wo_ref, wo, 128)

    def slot_e(yy, zz, kk):
        return enc.at[yy * 8 + zz * 2 + kk]

    enc_pair = send(enc_ref, slot_e(yl, z, k), slot_e(1 - yl, z, k), ypair)
    gq.x_start()
    gq.y_start(0)
    other = 1 - yh
    kv_far = [
        send(wk_ref, wk.at[p], wk.at[other * 4 + x], yfar),
        send(wv_ref, wv.at[p], wv.at[other * 4 + x], yfar),
    ]
    kv_own = kv_ring(wk_ref, wk, yh) + kv_ring(wv_ref, wv, yh)
    enc_sib = [send(enc_ref, slot_e(yl, z, k), slot_e(yl, z, 1 - k), sib)]
    enc_z = [
        send(enc_ref, slot_e(yl, z, k), slot_e(yl, step(z, -1), k), zup),
        send(enc_ref, slot_e(yl, z, k), slot_e(yl, step(z, 1), k), zdn),
    ]
    mask_z = [
        send(mask_ref, masks.at[z], masks.at[step(z, -1)], zup),
        send(mask_ref, masks.at[z], masks.at[step(z, 1)], zdn),
    ]

    load_x()

    def norm_rows(i, carry):
        part_rows = pl.ds(pl.multiple_of(i * 16, 16), 16)
        values = xbuf[part_rows, :].astype(F32)
        scale = lax.rsqrt(jnp.mean(values * values, axis=-1, keepdims=True) + 1e-06)
        rows[z, part_rows, :] = (values * scale).astype(BF16)
        return carry

    lax.fori_loop(0, 8, norm_rows, 0)
    rows_z = [
        send(rows.at[z], rows.at[z], rows.at[step(z, -1)], zup),
        send(rows.at[z], rows.at[z], rows.at[step(z, 1)], zdn),
    ]

    enc_pair()
    enc_sib.append(send(slot_e(1 - yl, z, k), slot_e(1 - yl, z, k), slot_e(1 - yl, z, 1 - k), sib))
    enc_zp = [
        send(slot_e(1 - yl, z, k), slot_e(1 - yl, z, k), slot_e(1 - yl, step(z, -1), k), zup),
        send(slot_e(1 - yl, z, k), slot_e(1 - yl, z, k), slot_e(1 - yl, step(z, 1), k), zdn),
    ]
    gq.x_forward()
    gq.y_start(1)
    gq.y_start(2)
    gq.y_forward(0)
    for got in kv_far:
        got()
    kv_oth = kv_ring(wk.at[other * 4 + x], wk, other) + kv_ring(wv.at[other * 4 + x], wv, other)
    gq.x_finish()
    gq.y_start(3)
    for got in kv_own:
        got()
    kv_fwd = kv_forward(wk, yh) + kv_forward(wv, yh)
    go.x_start()
    gq.y_finish(0)
    gq.y_forward(1)
    gq.y_forward(2)

    for got in mask_z:
        got()
    mask_far = send(masks.at[step(z, -1)], masks.at[step(z, -1)], masks.at[step(z, 2)], zup)
    for got in enc_z:
        got()
    lo, hi, far = step(z, -1), step(z, 1), step(z, 2)
    enc_far = [send(slot_e(yl, lo, k), slot_e(yl, lo, k), slot_e(yl, far, k), zup)]
    for zz in (lo, hi):
        enc_sib.append(send(slot_e(yl, zz, k), slot_e(yl, zz, k), slot_e(yl, zz, 1 - k), sib))
    for got in rows_z:
        got()
    a, b = pl.ds(0, 64), pl.ds(64, 64)
    rows_far = [
        send(rows.at[lo, a], rows.at[lo, a], rows.at[far, a], zup),
        send(rows.at[hi, b], rows.at[hi, b], rows.at[far, b], zdn),
    ]
    for got in enc_zp:
        got()
    enc_far.append(send(slot_e(1 - yl, hi, k), slot_e(1 - yl, hi, k), slot_e(1 - yl, far, k), zdn))
    for zz in (lo, hi):
        enc_sib.append(
            send(slot_e(1 - yl, zz, k), slot_e(1 - yl, zz, k), slot_e(1 - yl, zz, 1 - k), sib)
        )

    gq.y_finish(1)
    gq.y_finish(2)
    gq.y_forward(3)
    for got in kv_oth:
        got()
    kv_fwd += kv_forward(wk, other) + kv_forward(wv, other)
    go.x_forward()
    for got in enc_far:
        got()
    for yy in (yl, 1 - yl):
        enc_sib.append(send(slot_e(yy, far, k), slot_e(yy, far, k), slot_e(yy, far, 1 - k), sib))
    gq.y_finish(3)
    for wait in loads:
        wait()
    for got in kv_fwd + enc_sib:
        got()

    block = yl * 2 + k

    def project(w):
        total = jnp.zeros((256, 256), F32)
        for q in range(8):
            total += jnp.dot(
                enc[:, :, q * 512 : (q + 1) * 512].reshape(256, 512), w[q],
                preferred_element_type=F32,
            )
        return total

    kv[block, 0] = project(wk).T.astype(BF16)
    kv[block, 1] = project(wv).astype(BF16)
    kv_pair = send(kv.at[block], kv.at[block], kv.at[(1 - yl) * 2 + k], ypair)
    kv_sib = [send(kv.at[block], kv.at[block], kv.at[yl * 2 + 1 - k], sib)]
    go.y_start(0)
    go.y_start(1)
    go.y_start(2)
    go.x_finish()
    go.y_start(3)

    for got in rows_far:
        got()
    for i in range(4):
        gq.ready(i)

    def make_query(i, carry):
        blk, pair = i // 2, lax.rem(i, 2)
        total = jnp.zeros((256, 256), F32)
        for q in range(8):
            total += jnp.dot(
                rows[pl.ds(pair * 2, 2), :, q * 512 : (q + 1) * 512].reshape(256, 512),
                wq[q, blk],
                preferred_element_type=F32,
            )
        query[blk, pair] = total.astype(BF16)
        return carry

    lax.fori_loop(0, 8, make_query, 0)

    kv_pair()
    kv_sib.append(
        send(kv.at[(1 - yl) * 2 + k], kv.at[(1 - yl) * 2 + k], kv.at[(1 - yl) * 2 + 1 - k], sib)
    )
    go.y_forward(0)
    for got in kv_sib:
        got()
    mask_far()

    def spread(blk, carry):
        keys, values = kv[blk, 0], kv[blk, 1]
        for h in range(4):
            at_row = lax.broadcasted_iota(jnp.int32, (256, 256), 0) // 64 == h
            at_col = lax.broadcasted_iota(jnp.int32, (256, 256), 1) // 64 == h
            kmask[blk, h] = jnp.where(at_row, keys.astype(F32), 0.0).astype(BF16)
            vmask[blk, h] = jnp.where(at_col, values.astype(F32), 0.0).astype(BF16)
        return carry

    lax.fori_loop(0, 4, spread, 0)

    def attend(i, carry):
        blk, pair = i // 2, lax.rem(i, 2)
        left = query[blk, pair]
        open_keys = masks[pl.ds(pair * 2, 2), 0:1, :] > 0.5
        total = jnp.zeros((256, 256), F32)
        for h in range(4):
            scores = jnp.dot(left, kmask[blk, h], preferred_element_type=F32) * 0.125
            scores = jnp.where(open_keys, scores.reshape(2, 128, 256), -1e30)
            top = jnp.max(scores, axis=-1, keepdims=True)
            weights = jnp.exp(scores - top)
            probs = weights * pl.reciprocal(jnp.sum(weights, axis=-1, keepdims=True))
            total += jnp.dot(
                probs.astype(BF16).reshape(256, 256), vmask[blk, h], preferred_element_type=F32
            )
        ctx[blk, pair] = total.astype(BF16)
        return carry

    lax.fori_loop(0, 4, attend, 0)
    go.y_forward(1)
    lax.fori_loop(4, 8, attend, 0)

    got_t, got_f = {}, {}

    def column(j):
        return lax.rem(j, 2) * 4 + go.order[j // 2]

    def partial(j):
        col = column(j)

        def tile(i, carry):
            pair, side = i // 2, lax.rem(i, 2)
            lanes = pl.ds(pl.multiple_of(side * 256, 256), 256)
            total = jnp.zeros((256, 256), F32)
            for blk in range(4):
                total += jnp.dot(ctx[blk, pair], wo[col, blk, :, lanes], preferred_element_type=F32)
            part[j, pl.ds(pair * 2, 2), :, lanes] = total.reshape(2, 128, 256)
            return carry

        lax.fori_loop(0, 4, tile, 0)
        tsend[j, 0] = part[j, far, 0:64].astype(BF16)
        tsend[j, 1] = part[j, far, 64:128].astype(BF16)
        got_t[j] = [
            send(tsend.at[j, 0], trecv.at[j, 0], trecv.at[j, 0], zup),
            send(tsend.at[j, 1], trecv.at[j, 1], trecv.at[j, 1], zdn),
        ]

    def combine(j):
        for got in got_t[j]:
            got()
        fsend[j, 0, 0:64] = (part[j, hi, 0:64] + trecv[j, 0].astype(F32)).astype(BF16)
        fsend[j, 0, 64:128] = part[j, hi, 64:128].astype(BF16)
        fsend[j, 1, 0:64] = part[j, lo, 0:64].astype(BF16)
        fsend[j, 1, 64:128] = (part[j, lo, 64:128] + trecv[j, 1].astype(F32)).astype(BF16)
        got_f[j] = [
            send(fsend.at[j, 0], frecv.at[j, 0], frecv.at[j, 0], zup),
            send(fsend.at[j, 1], frecv.at[j, 1], frecv.at[j, 1], zdn),
        ]

    def finish(j):
        for got in got_f[j]:
            got()
        total = part[j, z] + frecv[j, 0].astype(F32) + frecv[j, 1].astype(F32)
        lanes = pl.ds(pl.multiple_of(column(j) * 512, 512), 512)
        out_ref[:, lanes] = total.astype(BF16)

    go.y_finish(0)
    go.y_forward(2)
    go.y_finish(1)
    for j in range(8):
        if j % 2 == 0:
            if j == 2:
                go.y_forward(3)
                go.y_finish(2)
            if j == 4:
                go.y_finish(3)
            go.ready(j // 2)
        partial(j)
        if j >= 1:
            combine(j - 1)
        if j >= 2:
            finish(j - 2)
    combine(7)
    finish(6)
    finish(7)
    for copy in sends:
        copy.wait_send()


def fused(x, enc, wq, wk, wv, wo, mask):
    vmem = pltpu.VMEM
    return pl.pallas_call(
        kernel,
        out_shape=jax.ShapeDtypeStruct((128, 4096), BF16),
        in_specs=[pl.BlockSpec(memory_space=pl.ANY)] * 7,
        out_specs=pl.BlockSpec(memory_space=pltpu.VMEM),
        scratch_shapes=[
            vmem((128, 4096), BF16),
            vmem((4, 128, 4096), BF16),
            vmem((4, 8, 256), F32),
            vmem((16, 16, 4096), BF16),
            vmem((8, 4, 512, 256), BF16),
            vmem((8, 512, 256), BF16),
            vmem((8, 512, 256), BF16),
            vmem((8, 4, 256, 512), BF16),
            vmem((4, 2, 256, 256), BF16),
            vmem((4, 4, 256, 256), BF16),
            vmem((4, 4, 256, 256), BF16),
            vmem((4, 2, 256, 256), BF16),
            vmem((4, 2, 256, 256), BF16),
            vmem((8, 4, 128, 512), F32),
            vmem((8, 2, 64, 512), BF16),
            vmem((8, 2, 64, 512), BF16),
            vmem((8, 2, 128, 512), BF16),
            vmem((8, 2, 128, 512), BF16),
            pltpu.SemaphoreType.DMA((MAX_COPIES,)),
            pltpu.SemaphoreType.DMA((MAX_COPIES,)),
            pltpu.SemaphoreType.DMA((8,)),
        ],
        compiler_params=pltpu.CompilerParams(
            collective_id=0, has_side_effects=True, vmem_limit_bytes=60 << 20
        ),
        name="cross_attention",
    )(x, enc, wq, wk, wv, wo, mask)


def shards(cand_states, enc_rows, w_query, w_key, w_value, w_out, tile_mask, counts):
    mask = jnp.broadcast_to(
        jnp.repeat(tile_mask[0, 0].astype(F32), 128)[None, :], (8, 256)
    )
    total = fused(cand_states[0, 0], enc_rows[0], w_query, w_key, w_value, w_out, mask)
    live = (lax.axis_index("cand") < counts[0]).astype(F32)
    return (total.astype(F32) * live).astype(BF16)[None, None]


def solution(mesh):
    return jax.shard_map(
        shards,
        mesh=mesh,
        in_specs=(
            P("prod", "cand", None, None),
            P("prod", "cand", None),
            P("prod", "cand"),
            P("prod", "cand"),
            P("prod", "cand"),
            P("cand", "prod"),
            P("prod", "cand", None),
            P("prod"),
        ),
        out_specs=P("prod", "cand", None, None),
        check_vma=False,
    )
```

```python
import functools

import jax
import jax.numpy as jnp
from jax import lax
from jax.experimental import pallas as pl
from jax.experimental.pallas import tpu as pltpu
from jax.sharding import PartitionSpec as P

MESH = pl.DeviceIdType.MESH
F32, BF16 = jnp.float32, jnp.bfloat16
MAX_COPIES = 192


def kernel(
    x_ref, enc_ref, wq_ref, wk_ref, wv_ref, wo_ref, mask_ref, count_ref,
    out_ref, xbuf, rows, masks, enc, wq, wk, wv, wo, kv, kvacc, kmask, vmask, qacc, query, ctx,
    part, tsend, trecv, fsend, frecv, send_sem, recv_sem, local_sem,
):
    p, c = lax.axis_index("prod"), lax.axis_index("cand")
    yh, x = p // 4, lax.rem(p, 4)
    yl, z, k = c // 8, lax.rem(c // 2, 4), lax.rem(c, 2)
    y = yh * 2 + yl
    step = lambda v, d: lax.rem(v + (d + 4), 4)

    def dev(yy, xx, zz, kk):
        return (yy // 2) * 4 + xx, lax.rem(yy, 2) * 8 + zz * 2 + kk

    sib = dev(y, x, z, 1 - k)
    xup, xdn = dev(y, step(x, 1), z, k), dev(y, step(x, -1), z, k)
    yup, ydn = dev(step(y, 1), x, z, k), dev(step(y, -1), x, z, k)
    yfar = dev(step(y, 2), x, z, k)
    ypair = dev(yh * 2 + 1 - yl, x, z, k)
    zup, zdn = dev(y, x, step(z, 1), k), dev(y, x, step(z, -1), k)

    barrier = pltpu.get_barrier_semaphore()
    peers = (sib, xup, xdn, yup, ydn, yfar, zup, zdn)
    for d in peers:
        pl.semaphore_signal(barrier, inc=1, device_id=d, device_id_type=MESH)

    count = [0]
    sends = []

    def send(src, there, here, d):
        i = count[0]
        count[0] += 1
        go = pltpu.make_async_remote_copy(
            src_ref=src, dst_ref=there, send_sem=send_sem.at[i], recv_sem=recv_sem.at[i],
            device_id=d, device_id_type=MESH,
        )
        go.start()
        sends.append(go)
        return pltpu.make_async_remote_copy(
            src_ref=src, dst_ref=here, send_sem=send_sem.at[i], recv_sem=recv_sem.at[i],
            device_id=d, device_id_type=MESH,
        ).wait_recv

    nlocal = [0]

    def local(src, dst):
        i = nlocal[0]
        nlocal[0] += 1
        copy = pltpu.make_async_copy(src, dst, local_sem.at[i])
        copy.start()
        return copy.wait

    load_x = local(x_ref, xbuf)
    loads = [
        local(wk_ref, wk.at[p]), local(wv_ref, wv.at[p]), local(enc_ref, enc.at[c]),
        local(wq_ref, wq.at[p, yl * 2 + k]), local(wo_ref, wo.at[p, yl * 2 + k]),
    ]
    pl.semaphore_wait(barrier, len(peers))

    class Plane:
        def __init__(self, src, buf, half):
            self.src, self.buf, self.half = src, buf, half
            self.order = (x, step(x, -1), step(x, 1), step(x, 2))
            self.got_y, self.got_far, self.got_sib = {}, {}, {i: [] for i in range(4)}

        def slot(self, yy, xx, kk):
            return self.buf.at[(yy // 2) * 4 + xx, lax.rem(yy, 2) * 2 + kk]

        def first(self, yy, xx):
            return self.slot(yy, xx, k).at[pl.ds(0, self.half)]

        def second(self, yy, xx):
            return self.slot(yy, xx, k).at[pl.ds(self.half, self.half)]

        def x_start(self):
            here = self.slot(y, x, k)
            self.got_x = [
                send(self.src, here, self.slot(y, step(x, -1), k), xup),
                send(self.src, here, self.slot(y, step(x, 1), k), xdn),
            ]

        def x_forward(self):
            for got in self.got_x:
                got()
            far = step(x, 2)
            lo, hi = step(x, -1), step(x, 1)
            self.got_xfar = [
                send(self.first(y, lo), self.first(y, lo), self.first(y, far), xup),
                send(self.second(y, hi), self.second(y, hi), self.second(y, far), xdn),
            ]

        def x_finish(self):
            for got in self.got_xfar:
                got()

        def cross(self, i, yy):
            xx = self.order[i]
            here = self.slot(yy, xx, k)
            src = self.src if i == 0 and yy is y else here
            self.got_sib[i].append(send(src, here, self.slot(yy, xx, 1 - k), sib))

        def y_start(self, i):
            xx = self.order[i]
            here = self.slot(y, xx, k)
            src = self.src if i == 0 else here
            self.got_y[i] = [
                send(src, here, self.slot(step(y, -1), xx, k), yup),
                send(src, here, self.slot(step(y, 1), xx, k), ydn),
            ]
            self.cross(i, y)

        def y_forward(self, i):
            xx = self.order[i]
            for got in self.got_y[i]:
                got()
            lo, hi, far = step(y, -1), step(y, 1), step(y, 2)
            self.got_far[i] = [
                send(self.first(lo, xx), self.first(lo, xx), self.first(far, xx), yup),
                send(self.second(hi, xx), self.second(hi, xx), self.second(far, xx), ydn),
            ]
            self.cross(i, lo)
            self.cross(i, hi)

        def y_finish(self, i):
            for got in self.got_far[i]:
                got()
            self.cross(i, step(y, 2))

        def ready(self, i):
            for got in self.got_sib[i]:
                got()

    def kv_ring(src, buf, g):
        here = buf.at[g * 4 + x]
        return [
            send(src, here, buf.at[g * 4 + step(x, -1)], xup),
            send(src, here, buf.at[g * 4 + step(x, 1)], xdn),
        ]

    def kv_forward(buf, g):
        lo, hi, far = (buf.at[g * 4 + step(x, d)] for d in (-1, 1, 2))
        a, b = pl.ds(0, 256), pl.ds(256, 256)
        return [
            send(lo.at[a], lo.at[a], far.at[a], xup),
            send(hi.at[b], hi.at[b], far.at[b], xdn),
        ]

    gq = Plane(wq_ref, wq, 256)
    go = Plane(wo_ref, wo, 128)

    def slot_e(yy, zz, kk):
        return enc.at[yy * 8 + zz * 2 + kk]

    enc_pair = send(enc_ref, slot_e(yl, z, k), slot_e(1 - yl, z, k), ypair)
    gq.x_start()
    other = 1 - yh
    kv_far = [
        send(wk_ref, wk.at[p], wk.at[other * 4 + x], yfar),
        send(wv_ref, wv.at[p], wv.at[other * 4 + x], yfar),
    ]
    gq.y_start(0)
    kv_own = kv_ring(wk_ref, wk, yh) + kv_ring(wv_ref, wv, yh)
    enc_z = [
        send(enc_ref, slot_e(yl, z, k), slot_e(yl, step(z, -1), k), zup),
        send(enc_ref, slot_e(yl, z, k), slot_e(yl, step(z, 1), k), zdn),
    ]
    enc_sib = [send(enc_ref, slot_e(yl, z, k), slot_e(yl, z, 1 - k), sib)]

    flags = mask_ref[...].astype(F32)
    lane = lax.broadcasted_iota(jnp.int32, (8, 256), 1)
    masks[z] = jnp.where(lane < 128, flags[:, 0:1], flags[:, 1:2])
    mask_z = [
        send(masks.at[z], masks.at[z], masks.at[step(z, -1)], zup),
        send(masks.at[z], masks.at[z], masks.at[step(z, 1)], zdn),
    ]

    load_x()

    def norm_rows(i, carry):
        part_rows = pl.ds(pl.multiple_of(i * 16, 16), 16)
        values = xbuf[part_rows, :].astype(F32)
        scale = lax.rsqrt(jnp.mean(values * values, axis=-1, keepdims=True) + 1e-06)
        rows[z, part_rows, :] = (values * scale).astype(BF16)
        return carry

    lax.fori_loop(0, 8, norm_rows, 0)
    rows_z = [
        send(rows.at[z], rows.at[z], rows.at[step(z, -1)], zup),
        send(rows.at[z], rows.at[z], rows.at[step(z, 1)], zdn),
    ]

    enc_pair()
    enc_sib.append(send(slot_e(1 - yl, z, k), slot_e(1 - yl, z, k), slot_e(1 - yl, z, 1 - k), sib))
    enc_zp = [
        send(slot_e(1 - yl, z, k), slot_e(1 - yl, z, k), slot_e(1 - yl, step(z, -1), k), zup),
        send(slot_e(1 - yl, z, k), slot_e(1 - yl, z, k), slot_e(1 - yl, step(z, 1), k), zdn),
    ]
    gq.x_forward()
    gq.y_start(1)
    gq.y_start(2)
    for got in kv_far:
        got()
    kv_oth = kv_ring(wk.at[other * 4 + x], wk, other) + kv_ring(wv.at[other * 4 + x], wv, other)
    gq.y_forward(0)
    for got in kv_own:
        got()
    kv_fwd = kv_forward(wk, yh) + kv_forward(wv, yh)
    gq.x_finish()
    gq.y_start(3)

    for got in mask_z:
        got()
    mask_far = send(masks.at[step(z, -1)], masks.at[step(z, -1)], masks.at[step(z, 2)], zup)
    for got in enc_z:
        got()
    lo, hi, far = step(z, -1), step(z, 1), step(z, 2)
    enc_far = [send(slot_e(yl, lo, k), slot_e(yl, lo, k), slot_e(yl, far, k), zup)]
    for zz in (lo, hi):
        enc_sib.append(send(slot_e(yl, zz, k), slot_e(yl, zz, k), slot_e(yl, zz, 1 - k), sib))
    gq.y_finish(0)
    gq.y_forward(1)
    for got in enc_zp:
        got()
    enc_far.append(send(slot_e(1 - yl, hi, k), slot_e(1 - yl, hi, k), slot_e(1 - yl, far, k), zdn))
    for zz in (lo, hi):
        enc_sib.append(
            send(slot_e(1 - yl, zz, k), slot_e(1 - yl, zz, k), slot_e(1 - yl, zz, 1 - k), sib)
        )
    for got in rows_z:
        got()
    a, b = pl.ds(0, 64), pl.ds(64, 64)
    rows_far = [
        send(rows.at[lo, a], rows.at[lo, a], rows.at[far, a], zup),
        send(rows.at[hi, b], rows.at[hi, b], rows.at[far, b], zdn),
    ]
    gq.y_forward(2)
    for got in kv_oth:
        got()
    kv_last = kv_forward(wk, other) + kv_forward(wv, other)
    gq.y_finish(1)
    gq.y_forward(3)
    for got in enc_far:
        got()
    for yy in (yl, 1 - yl):
        enc_sib.append(send(slot_e(yy, far, k), slot_e(yy, far, k), slot_e(yy, far, 1 - k), sib))
    go.x_start()
    gq.y_finish(2)

    block = yl * 2 + k

    def project(q, fresh=False):
        lanes = pl.ds(pl.multiple_of(q * 512, 512), 512)
        left = enc[:, :, lanes].reshape(256, 512)
        for i, w in enumerate((wk, wv)):
            term = jnp.dot(left, w[q], preferred_element_type=F32)
            kvacc[i] = term if fresh else kvacc[i] + term

    for wait in loads:
        wait()
    for got in kv_fwd + enc_sib:
        got()
    project(yh * 4 + x, fresh=True)
    for d in (-1, 1, 2):
        project(yh * 4 + step(x, d))
    for d in (0, -1, 1):
        project(other * 4 + step(x, d))

    for got in rows_far:
        got()

    def add_query(chunks, fresh, last):
        def tile(i, carry):
            blk, pair = i // 2, lax.rem(i, 2)
            total = jnp.zeros((256, 256), F32) if fresh else qacc[blk, pair]
            for xx in chunks:
                for q in (xx, 4 + xx):
                    lanes = pl.ds(pl.multiple_of(q * 512, 512), 512)
                    total += jnp.dot(
                        rows[pl.ds(pair * 2, 2), :, lanes].reshape(256, 512), wq[q, blk],
                        preferred_element_type=F32,
                    )
            if last:
                query[blk, pair] = total.astype(BF16)
            else:
                qacc[blk, pair] = total
            return carry

        lax.fori_loop(0, 8, tile, 0)

    for i in range(3):
        gq.ready(i)
    add_query(gq.order[:3], True, False)

    for got in kv_last:
        got()
    project(other * 4 + step(x, 2))
    kv[block, 0] = kvacc[0].T.astype(BF16)
    kv[block, 1] = kvacc[1].astype(BF16)
    kv_pair = send(kv.at[block], kv.at[block], kv.at[(1 - yl) * 2 + k], ypair)
    kv_sib = [
        send(kv.at[block], kv.at[block], kv.at[yl * 2 + 1 - k], sib),
    ]
    gq.y_finish(3)
    go.y_start(0)
    go.x_forward()
    go.y_start(1)
    gq.ready(3)
    add_query(gq.order[3:], False, True)
    mask_far()

    def attend(blk):
        keys, values = kv[blk, 0].astype(F32), kv[blk, 1].astype(F32)
        for h in range(4):
            at_row = lax.broadcasted_iota(jnp.int32, (256, 256), 0) // 64 == h
            at_col = lax.broadcasted_iota(jnp.int32, (256, 256), 1) // 64 == h
            kmask[h] = jnp.where(at_row, keys, 0.0).astype(BF16)
            vmask[h] = jnp.where(at_col, values, 0.0).astype(BF16)

        def tile(pair, carry):
            left = query[blk, pair]
            open_keys = masks[pl.ds(pair * 2, 2), 0:1, :] > 0.5
            total = jnp.zeros((256, 256), F32)
            for h in range(4):
                scores = jnp.dot(left, kmask[h], preferred_element_type=F32) * 0.125
                scores = jnp.where(open_keys, scores.reshape(2, 128, 256), -1e30)
                top = jnp.max(scores, axis=-1, keepdims=True)
                weights = jnp.exp(scores - top)
                probs = weights * pl.reciprocal(jnp.sum(weights, axis=-1, keepdims=True))
                total += jnp.dot(
                    probs.astype(BF16).reshape(256, 256), vmask[h], preferred_element_type=F32
                )
            ctx[blk, pair] = total.astype(BF16)
            return carry

        lax.fori_loop(0, 2, tile, 0)

    attend(block)
    kv_sib[0]()
    attend(yl * 2 + 1 - k)
    go.x_finish()
    kv_pair()
    kv_sib.append(
        send(kv.at[(1 - yl) * 2 + k], kv.at[(1 - yl) * 2 + k], kv.at[(1 - yl) * 2 + 1 - k], sib)
    )
    go.y_forward(0)
    go.y_start(2)
    attend((1 - yl) * 2 + k)
    kv_sib[1]()
    attend((1 - yl) * 2 + 1 - k)

    got_t, got_f = {}, {}
    live = (c < count_ref[...]).astype(F32)

    def column(j):
        return lax.rem(j, 2) * 4 + go.order[j // 2]

    def partial(j):
        col = column(j)

        def tile(i, carry):
            pair, side = i // 2, lax.rem(i, 2)
            lanes = pl.ds(pl.multiple_of(side * 256, 256), 256)
            total = jnp.zeros((256, 256), F32)
            for blk in range(4):
                total += jnp.dot(ctx[blk, pair], wo[col, blk, :, lanes], preferred_element_type=F32)
            part[j, pl.ds(pair * 2, 2), :, lanes] = total.reshape(2, 128, 256)
            return carry

        lax.fori_loop(0, 4, tile, 0)
        tsend[j, 0] = part[j, far, 0:64].astype(BF16)
        tsend[j, 1] = part[j, far, 64:128].astype(BF16)
        got_t[j] = [
            send(tsend.at[j, 0], trecv.at[j, 0], trecv.at[j, 0], zup),
            send(tsend.at[j, 1], trecv.at[j, 1], trecv.at[j, 1], zdn),
        ]

    def combine(j):
        for got in got_t[j]:
            got()
        fsend[j, 0, 0:64] = (part[j, hi, 0:64] + trecv[j, 0].astype(F32)).astype(BF16)
        fsend[j, 0, 64:128] = part[j, hi, 64:128].astype(BF16)
        fsend[j, 1, 0:64] = part[j, lo, 0:64].astype(BF16)
        fsend[j, 1, 64:128] = (part[j, lo, 64:128] + trecv[j, 1].astype(F32)).astype(BF16)
        got_f[j] = [
            send(fsend.at[j, 0], frecv.at[j, 0], frecv.at[j, 0], zup),
            send(fsend.at[j, 1], frecv.at[j, 1], frecv.at[j, 1], zdn),
        ]

    def finish(j):
        for got in got_f[j]:
            got()
        total = part[j, z] + frecv[j, 0].astype(F32) + frecv[j, 1].astype(F32)
        lanes = pl.ds(pl.multiple_of(column(j) * 512, 512), 512)
        out_ref[:, lanes] = (total * live).astype(BF16)

    for j in range(8):
        i = j // 2
        if j % 2 == 0:
            go.y_finish(i)
            if i < 3:
                go.y_forward(i + 1)
            if i < 1:
                go.y_start(3)
            go.ready(i)
        partial(j)
        if j >= 1:
            combine(j - 1)
        if j >= 2:
            finish(j - 2)
    combine(7)
    finish(6)
    finish(7)
    for copy in sends:
        copy.wait_send()


def fused(x, enc, wq, wk, wv, wo, mask, count):
    vmem = pltpu.VMEM
    return pl.pallas_call(
        kernel,
        out_shape=jax.ShapeDtypeStruct((128, 4096), BF16),
        in_specs=[pl.BlockSpec(memory_space=pl.ANY)] * 6
        + [pl.BlockSpec(memory_space=pltpu.VMEM)] * 2,
        out_specs=pl.BlockSpec(memory_space=pltpu.VMEM),
        scratch_shapes=[
            vmem((128, 4096), BF16),
            vmem((4, 128, 4096), BF16),
            vmem((4, 8, 256), F32),
            vmem((16, 16, 4096), BF16),
            vmem((8, 4, 512, 256), BF16),
            vmem((8, 512, 256), BF16),
            vmem((8, 512, 256), BF16),
            vmem((8, 4, 256, 512), BF16),
            vmem((4, 2, 256, 256), BF16),
            vmem((2, 256, 256), F32),
            vmem((4, 256, 256), BF16),
            vmem((4, 256, 256), BF16),
            vmem((4, 2, 256, 256), F32),
            vmem((4, 2, 256, 256), BF16),
            vmem((4, 2, 256, 256), BF16),
            vmem((8, 4, 128, 512), F32),
            vmem((8, 2, 64, 512), BF16),
            vmem((8, 2, 64, 512), BF16),
            vmem((8, 2, 128, 512), BF16),
            vmem((8, 2, 128, 512), BF16),
            pltpu.SemaphoreType.DMA((MAX_COPIES,)),
            pltpu.SemaphoreType.DMA((MAX_COPIES,)),
            pltpu.SemaphoreType.DMA((8,)),
        ],
        compiler_params=pltpu.CompilerParams(
            collective_id=0, has_side_effects=True, vmem_limit_bytes=60 << 20
        ),
        name="cross_attention",
    )(x, enc, wq, wk, wv, wo, mask, count)


def shards(cand_states, enc_rows, w_query, w_key, w_value, w_out, tile_mask, counts):
    total = fused(
        cand_states[0, 0], enc_rows[0], w_query, w_key, w_value, w_out, tile_mask[0], counts[None]
    )
    return total[None, None]


def solution(mesh):
    return jax.shard_map(
        shards,
        mesh=mesh,
        in_specs=(
            P("prod", "cand", None, None),
            P("prod", "cand", None),
            P("prod", "cand"),
            P("prod", "cand"),
            P("prod", "cand"),
            P("cand", "prod"),
            P("prod", "cand", None),
            P("prod"),
        ),
        out_specs=P("prod", "cand", None, None),
        check_vma=False,
    )
```

```python
import functools

import jax
import jax.numpy as jnp
from jax import lax
from jax.experimental import pallas as pl
from jax.experimental.pallas import tpu as pltpu
from jax.sharding import PartitionSpec as P

MESH = pl.DeviceIdType.MESH
F32, BF16 = jnp.float32, jnp.bfloat16
MAX_COPIES = 224


def kernel(
    x_ref, enc_ref, wq_ref, wk_ref, wv_ref, wo_ref, mask_ref, count_ref,
    out_ref, xbuf, rows, masks, enc, wq, wk, wv, wo, kv, kvacc, kmask, vmask, qacc, query, ctx,
    tsend, trecv, fsend, frecv, send_sem, recv_sem, local_sem,
):
    p, c = lax.axis_index("prod"), lax.axis_index("cand")
    yh, x = p // 4, lax.rem(p, 4)
    yl, z, k = c // 8, lax.rem(c // 2, 4), lax.rem(c, 2)
    y = yh * 2 + yl
    step = lambda v, d: lax.rem(v + (d + 4), 4)

    def dev(yy, xx, zz, kk):
        return (yy // 2) * 4 + xx, lax.rem(yy, 2) * 8 + zz * 2 + kk

    sib = dev(y, x, z, 1 - k)
    xup, xdn = dev(y, step(x, 1), z, k), dev(y, step(x, -1), z, k)
    yup, ydn = dev(step(y, 1), x, z, k), dev(step(y, -1), x, z, k)
    yfar = dev(step(y, 2), x, z, k)
    ypair = dev(yh * 2 + 1 - yl, x, z, k)
    zup, zdn = dev(y, x, step(z, 1), k), dev(y, x, step(z, -1), k)

    barrier = pltpu.get_barrier_semaphore()
    peers = (sib, xup, xdn, yup, ydn, yfar, zup, zdn)
    for d in peers:
        pl.semaphore_signal(barrier, inc=1, device_id=d, device_id_type=MESH)

    sends = []

    def send(src, there, here, d):
        i = len(sends)
        go = pltpu.make_async_remote_copy(
            src_ref=src, dst_ref=there, send_sem=send_sem.at[i], recv_sem=recv_sem.at[i],
            device_id=d, device_id_type=MESH,
        )
        go.start()
        sends.append(go)
        return pltpu.make_async_remote_copy(
            src_ref=src, dst_ref=here, send_sem=send_sem.at[i], recv_sem=recv_sem.at[i],
            device_id=d, device_id_type=MESH,
        ).wait_recv

    nlocal = [0]

    def local(src, dst):
        i = nlocal[0]
        nlocal[0] += 1
        copy = pltpu.make_async_copy(src, dst, local_sem.at[i])
        copy.start()
        return copy.wait

    load_x = local(x_ref, xbuf)
    loads = [
        local(wk_ref, wk.at[p]), local(wv_ref, wv.at[p]), local(enc_ref, enc.at[c]),
        local(wq_ref, wq.at[p, yl * 2 + k]),
        local(wo_ref.at[:, pl.ds(0, 256)], wo.at[0, p, yl * 2 + k]),
        local(wo_ref.at[:, pl.ds(256, 256)], wo.at[1, p, yl * 2 + k]),
    ]

    flags = mask_ref[...].astype(F32)
    lane = lax.broadcasted_iota(jnp.int32, (8, 256), 1)
    masks[z] = jnp.where(lane < 128, flags[:, 0:1], flags[:, 1:2])

    load_x()

    def norm_rows(i, carry):
        part_rows = pl.ds(pl.multiple_of(i * 16, 16), 16)
        values = xbuf[part_rows, :].astype(F32)
        scale = lax.rsqrt(jnp.mean(values * values, axis=-1, keepdims=True) + 1e-06)
        rows[z, part_rows, :] = (values * scale).astype(BF16)
        return carry

    lax.fori_loop(0, 8, norm_rows, 0)
    pl.semaphore_wait(barrier, len(peers))

    class Plane:
        def __init__(self, src, buf, x_first, order):
            self.src, self.buf, self.x_first, self.order = src, buf, x_first, order
            self.half = buf.shape[2] // 2
            self.a, self.b = (x, y) if x_first else (y, x)
            self.aup, self.adn = (xup, xdn) if x_first else (yup, ydn)
            self.bup, self.bdn = (yup, ydn) if x_first else (xup, xdn)
            self.got_b, self.got_far, self.got_sib = {}, {}, {i: [] for i in range(4)}

        def slot(self, aa, bb, kk):
            yy, xx = (bb, aa) if self.x_first else (aa, bb)
            return self.buf.at[(yy // 2) * 4 + xx, lax.rem(yy, 2) * 2 + kk]

        def first(self, aa, bb):
            return self.slot(aa, bb, k).at[pl.ds(0, self.half)]

        def second(self, aa, bb):
            return self.slot(aa, bb, k).at[pl.ds(self.half, self.half)]

        def a_start(self):
            here = self.slot(self.a, self.b, k)
            self.got_a = [
                send(self.src, here, self.slot(step(self.a, -1), self.b, k), self.aup),
                send(self.src, here, self.slot(step(self.a, 1), self.b, k), self.adn),
            ]

        def a_forward(self):
            for got in self.got_a:
                got()
            lo, hi, far = (step(self.a, d) for d in (-1, 1, 2))
            self.got_afar = [
                send(self.first(lo, self.b), self.first(lo, self.b), self.first(far, self.b), self.aup),
                send(self.second(hi, self.b), self.second(hi, self.b), self.second(far, self.b), self.adn),
            ]

        def a_finish(self):
            for got in self.got_afar:
                got()

        def cross(self, i, bb, src=None):
            aa = self.order[i]
            here = self.slot(aa, bb, k)
            self.got_sib[i].append(
                send(here if src is None else src, here, self.slot(aa, bb, 1 - k), sib)
            )

        def b_start(self, i):
            aa = self.order[i]
            here = self.slot(aa, self.b, k)
            src = self.src if i == 0 else here
            self.got_b[i] = [
                send(src, here, self.slot(aa, step(self.b, -1), k), self.bup),
                send(src, here, self.slot(aa, step(self.b, 1), k), self.bdn),
            ]
            self.cross(i, self.b, src)

        def b_forward(self, i):
            aa = self.order[i]
            for got in self.got_b[i]:
                got()
            lo, hi, far = (step(self.b, d) for d in (-1, 1, 2))
            self.got_far[i] = [
                send(self.first(aa, lo), self.first(aa, lo), self.first(aa, far), self.bup),
                send(self.second(aa, hi), self.second(aa, hi), self.second(aa, far), self.bdn),
            ]
            self.cross(i, lo)
            self.cross(i, hi)

        def b_finish(self, i):
            for got in self.got_far[i]:
                got()
            self.cross(i, step(self.b, 2))

        def ready(self, i):
            for got in self.got_sib[i]:
                got()

    def kv_ring(src, buf, g):
        here = buf.at[g * 4 + x]
        return [
            send(src, here, buf.at[g * 4 + step(x, -1)], xup),
            send(src, here, buf.at[g * 4 + step(x, 1)], xdn),
        ]

    def kv_forward(buf, g):
        lo, hi, far = (buf.at[g * 4 + step(x, d)] for d in (-1, 1, 2))
        a, b = pl.ds(0, 256), pl.ds(256, 256)
        return [
            send(lo.at[a], lo.at[a], far.at[a], xup),
            send(hi.at[b], hi.at[b], far.at[b], xdn),
        ]

    xs = (x, step(x, -1), step(x, 1), step(x, 2))
    y2 = yh * 2 + 1 - yl
    ys = (y, y2, step(y, 2), step(y2, 2))
    gq = Plane(wq_ref, wq, True, xs)
    ga = Plane(wo_ref.at[:, pl.ds(0, 256)], wo.at[0], True, xs)
    gb = Plane(wo_ref.at[:, pl.ds(256, 256)], wo.at[1], False, ys)

    def slot_e(yy, zz, kk):
        return enc.at[yy * 8 + zz * 2 + kk]

    enc_pair = send(enc_ref, slot_e(yl, z, k), slot_e(1 - yl, z, k), ypair)
    gq.a_start()
    other = 1 - yh
    kv_far = [
        send(wk_ref, wk.at[p], wk.at[other * 4 + x], yfar),
        send(wv_ref, wv.at[p], wv.at[other * 4 + x], yfar),
    ]
    gq.b_start(0)
    kv_own = kv_ring(wk_ref, wk, yh) + kv_ring(wv_ref, wv, yh)
    enc_z = [
        send(enc_ref, slot_e(yl, z, k), slot_e(yl, step(z, -1), k), zup),
        send(enc_ref, slot_e(yl, z, k), slot_e(yl, step(z, 1), k), zdn),
    ]
    rows_z = [
        send(rows.at[z], rows.at[z], rows.at[step(z, -1)], zup),
        send(rows.at[z], rows.at[z], rows.at[step(z, 1)], zdn),
    ]
    mask_z = [
        send(masks.at[z], masks.at[z], masks.at[step(z, -1)], zup),
        send(masks.at[z], masks.at[z], masks.at[step(z, 1)], zdn),
    ]
    enc_sib = [send(enc_ref, slot_e(yl, z, k), slot_e(yl, z, 1 - k), sib)]
    lo, hi, far = step(z, -1), step(z, 1), step(z, 2)

    enc_pair()
    enc_sib.append(send(slot_e(1 - yl, z, k), slot_e(1 - yl, z, k), slot_e(1 - yl, z, 1 - k), sib))
    enc_zp = [
        send(slot_e(1 - yl, z, k), slot_e(1 - yl, z, k), slot_e(1 - yl, lo, k), zup),
        send(slot_e(1 - yl, z, k), slot_e(1 - yl, z, k), slot_e(1 - yl, hi, k), zdn),
    ]
    gq.a_forward()
    gq.b_start(1)
    gq.b_start(2)
    for got in kv_far:
        got()
    kv_oth = kv_ring(wk.at[other * 4 + x], wk, other) + kv_ring(wv.at[other * 4 + x], wv, other)
    gq.b_forward(0)
    for got in kv_own:
        got()
    kv_fwd = kv_forward(wk, yh) + kv_forward(wv, yh)
    gq.a_finish()
    gq.b_start(3)

    for got in mask_z:
        got()
    mask_far = send(masks.at[lo], masks.at[lo], masks.at[far], zup)
    for got in enc_z:
        got()
    enc_far = [send(slot_e(yl, lo, k), slot_e(yl, lo, k), slot_e(yl, far, k), zup)]
    for zz in (lo, hi):
        enc_sib.append(send(slot_e(yl, zz, k), slot_e(yl, zz, k), slot_e(yl, zz, 1 - k), sib))
    for got in enc_zp:
        got()
    enc_far.append(send(slot_e(1 - yl, hi, k), slot_e(1 - yl, hi, k), slot_e(1 - yl, far, k), zdn))
    for zz in (lo, hi):
        enc_sib.append(
            send(slot_e(1 - yl, zz, k), slot_e(1 - yl, zz, k), slot_e(1 - yl, zz, 1 - k), sib)
        )
    for got in rows_z:
        got()
    top, low = pl.ds(0, 64), pl.ds(64, 64)
    rows_far = [
        send(rows.at[lo, top], rows.at[lo, top], rows.at[far, top], zup),
        send(rows.at[hi, low], rows.at[hi, low], rows.at[far, low], zdn),
    ]
    gq.b_forward(1)
    for got in kv_oth:
        got()
    kv_last = kv_forward(wk, other) + kv_forward(wv, other)
    ga.a_start()
    gq.b_forward(2)
    for got in enc_far:
        got()
    for yy in (yl, 1 - yl):
        enc_sib.append(send(slot_e(yy, far, k), slot_e(yy, far, k), slot_e(yy, far, 1 - k), sib))
    gq.b_finish(0)
    gq.b_forward(3)
    gb.a_start()
    ga.b_start(0)

    block = yl * 2 + k

    def project(q, fresh=False):
        lanes = pl.ds(pl.multiple_of(q * 512, 512), 512)
        left = enc[:, :, lanes].reshape(256, 512)
        for i, w in enumerate((wk, wv)):
            term = jnp.dot(left, w[q], preferred_element_type=F32)
            kvacc[i] = term if fresh else kvacc[i] + term

    def add_query(xx, fresh=False, last=False):
        def tile(blk, carry):
            total = jnp.zeros((512, 256), F32) if fresh else qacc[blk]
            for q in (xx, 4 + xx):
                lanes = pl.ds(pl.multiple_of(q * 512, 512), 512)
                total += jnp.dot(
                    rows[:, :, lanes].reshape(512, 512), wq[q, blk], preferred_element_type=F32
                )
            if last:
                query[blk] = total.astype(BF16).reshape(4, 128, 256)
            else:
                qacc[blk] = total
            return carry

        lax.fori_loop(0, 4, tile, 0)

    for wait in loads:
        wait()
    for got in kv_fwd + enc_sib:
        got()
    project(yh * 4 + x, fresh=True)
    for d in (-1, 1, 2):
        project(yh * 4 + step(x, d))
    for d in (0, -1, 1):
        project(other * 4 + step(x, d))
    gq.b_finish(1)
    for got in rows_far:
        got()
    gq.ready(0)
    add_query(xs[0], fresh=True)
    for got in kv_last:
        got()
    ga.a_forward()
    project(other * 4 + step(x, 2))
    kv[block, 0] = kvacc[0].T.astype(BF16)
    kv[block, 1] = kvacc[1].astype(BF16)
    kv_pair = send(kv.at[block], kv.at[block], kv.at[(1 - yl) * 2 + k], ypair)
    kv_sib = [send(kv.at[block], kv.at[block], kv.at[yl * 2 + 1 - k], sib)]
    gb.b_start(0)
    gq.b_finish(2)
    gq.ready(1)
    add_query(xs[1])
    gq.b_finish(3)
    ga.b_start(1)
    gb.a_forward()
    gb.b_start(1)
    gq.ready(2)
    add_query(xs[2])
    ga.a_finish()
    kv_pair()
    kv_sib.append(
        send(kv.at[(1 - yl) * 2 + k], kv.at[(1 - yl) * 2 + k], kv.at[(1 - yl) * 2 + 1 - k], sib)
    )
    ga.b_forward(0)
    gq.ready(3)
    add_query(xs[3], last=True)
    mask_far()
    for got in kv_sib:
        got()

    def spread(blk, carry):
        keys, values = kv[blk, 0].astype(F32), kv[blk, 1].astype(F32)
        for h in range(4):
            at_row = lax.broadcasted_iota(jnp.int32, (256, 256), 0) // 64 == h
            at_col = lax.broadcasted_iota(jnp.int32, (256, 256), 1) // 64 == h
            kmask[blk, h] = jnp.where(at_row, keys, 0.0).astype(BF16)
            vmask[blk, h] = jnp.where(at_col, values, 0.0).astype(BF16)
        return carry

    lax.fori_loop(0, 4, spread, 0)
    gb.a_finish()
    gb.b_forward(0)
    ga.b_finish(0)

    def attend(cand):
        open_keys = masks[cand, 0:1, :] > 0.5

        def tile(blk, carry):
            left = query[blk, cand]
            total = jnp.zeros((128, 256), F32)
            for h in range(4):
                scores = jnp.dot(left, kmask[blk, h], preferred_element_type=F32) * 0.125
                scores = jnp.where(open_keys, scores, -1e30)
                best = jnp.max(scores, axis=-1, keepdims=True)
                weights = jnp.exp(scores - best)
                probs = weights * pl.reciprocal(jnp.sum(weights, axis=-1, keepdims=True))
                total += jnp.dot(probs.astype(BF16), vmask[blk, h], preferred_element_type=F32)
            ctx[cand, blk] = total.astype(BF16)
            return carry

        lax.fori_loop(0, 4, tile, 0)

    got_t, got_f = {}, {}
    live = (c < count_ref[...]).astype(F32)

    def columns(j, h):
        if j < 4:
            return 0, h * 4 + xs[j]
        g = yh if j < 6 else other
        return 1, g * 4 + xs[(j % 2) * 2 + h]

    def product(cand, j, h):
        side, q = columns(j, h)
        total = jnp.zeros((128, 256), F32)
        for blk in range(4):
            total += jnp.dot(ctx[cand, blk], wo[side, q, blk], preferred_element_type=F32)
        return total

    def start_sums(j):
        for h in range(2):
            lanes = pl.ds(h * 256, 256)
            total = product(far, j, h).astype(BF16)
            tsend[j, 0, :, lanes] = total[0:64]
            tsend[j, 1, :, lanes] = total[64:128]
        got_t[j] = [
            send(tsend.at[j, 0], trecv.at[j, 0], trecv.at[j, 0], zup),
            send(tsend.at[j, 1], trecv.at[j, 1], trecv.at[j, 1], zdn),
        ]

    def pass_sums(j):
        for got in got_t[j]:
            got()
        for h in range(2):
            lanes = pl.ds(h * 256, 256)
            up, dn = product(hi, j, h), product(lo, j, h)
            fsend[j, 0, 0:64, lanes] = (up[0:64] + trecv[j, 0, :, lanes].astype(F32)).astype(BF16)
            fsend[j, 0, 64:128, lanes] = up[64:128].astype(BF16)
            fsend[j, 1, 0:64, lanes] = dn[0:64].astype(BF16)
            fsend[j, 1, 64:128, lanes] = (dn[64:128] + trecv[j, 1, :, lanes].astype(F32)).astype(BF16)
        got_f[j] = [
            send(fsend.at[j, 0], frecv.at[j, 0], frecv.at[j, 0], zup),
            send(fsend.at[j, 1], frecv.at[j, 1], frecv.at[j, 1], zdn),
        ]

    def end_sums(j):
        for got in got_f[j]:
            got()
        for h in range(2):
            lanes = pl.ds(h * 256, 256)
            total = product(z, j, h) + frecv[j, 0, :, lanes].astype(F32) + frecv[j, 1, :, lanes].astype(F32)
            side, q = columns(j, h)
            out_ref[:, pl.ds(pl.multiple_of(q * 512 + side * 256, 256), 256)] = (total * live).astype(BF16)

    attend(far)
    ga.b_start(2)
    ga.b_forward(1)
    ga.ready(0)
    start_sums(0)
    gb.b_forward(1)
    gb.b_start(2)
    attend(hi)
    gb.b_finish(0)
    ga.b_finish(1)
    ga.b_start(3)
    ga.ready(1)
    start_sums(1)
    attend(lo)
    pass_sums(0)
    ga.b_forward(2)
    gb.b_finish(1)
    gb.b_start(3)
    attend(z)
    ga.b_finish(2)
    ga.ready(2)
    start_sums(2)
    pass_sums(1)
    ga.b_forward(3)
    gb.b_forward(2)
    ga.b_finish(3)
    ga.ready(3)
    start_sums(3)
    pass_sums(2)
    end_sums(0)
    gb.ready(0)
    gb.ready(1)
    gb.b_finish(2)
    gb.b_forward(3)
    start_sums(4)
    start_sums(5)
    pass_sums(3)
    end_sums(1)
    gb.b_finish(3)
    pass_sums(4)
    end_sums(2)
    gb.ready(2)
    gb.ready(3)
    start_sums(6)
    start_sums(7)
    pass_sums(5)
    end_sums(3)
    pass_sums(6)
    pass_sums(7)
    for j in range(4, 8):
        end_sums(j)
    for copy in sends:
        copy.wait_send()


def fused(x, enc, wq, wk, wv, wo, mask, count):
    vmem = pltpu.VMEM
    return pl.pallas_call(
        kernel,
        out_shape=jax.ShapeDtypeStruct((128, 4096), BF16),
        in_specs=[pl.BlockSpec(memory_space=pl.ANY)] * 6
        + [pl.BlockSpec(memory_space=pltpu.VMEM)] * 2,
        out_specs=pl.BlockSpec(memory_space=pltpu.VMEM),
        scratch_shapes=[
            vmem((128, 4096), BF16),
            vmem((4, 128, 4096), BF16),
            vmem((4, 8, 256), F32),
            vmem((16, 16, 4096), BF16),
            vmem((8, 4, 512, 256), BF16),
            vmem((8, 512, 256), BF16),
            vmem((8, 512, 256), BF16),
            vmem((2, 8, 4, 256, 256), BF16),
            vmem((4, 2, 256, 256), BF16),
            vmem((2, 256, 256), F32),
            vmem((4, 4, 256, 256), BF16),
            vmem((4, 4, 256, 256), BF16),
            vmem((4, 512, 256), F32),
            vmem((4, 4, 128, 256), BF16),
            vmem((4, 4, 128, 256), BF16),
            vmem((8, 2, 64, 512), BF16),
            vmem((8, 2, 64, 512), BF16),
            vmem((8, 2, 128, 512), BF16),
            vmem((8, 2, 128, 512), BF16),
            pltpu.SemaphoreType.DMA((MAX_COPIES,)),
            pltpu.SemaphoreType.DMA((MAX_COPIES,)),
            pltpu.SemaphoreType.DMA((8,)),
        ],
        compiler_params=pltpu.CompilerParams(
            collective_id=0, has_side_effects=True, vmem_limit_bytes=60 << 20
        ),
        name="cross_attention",
    )(x, enc, wq, wk, wv, wo, mask, count)


def shards(cand_states, enc_rows, w_query, w_key, w_value, w_out, tile_mask, counts):
    total = fused(
        cand_states[0, 0], enc_rows[0], w_query, w_key, w_value, w_out, tile_mask[0], counts[None]
    )
    return total[None, None]


def solution(mesh):
    return jax.shard_map(
        shards,
        mesh=mesh,
        in_specs=(
            P("prod", "cand", None, None),
            P("prod", "cand", None),
            P("prod", "cand"),
            P("prod", "cand"),
            P("prod", "cand"),
            P("cand", "prod"),
            P("prod", "cand", None),
            P("prod"),
        ),
        out_specs=P("prod", "cand", None, None),
        check_vma=False,
    )
```

```python
import math

import jax
import jax.numpy as jnp
from jax import lax
from jax.experimental import pallas as pl
from jax.experimental.pallas import tpu as pltpu
from jax.sharding import PartitionSpec as P

MESH = pl.DeviceIdType.MESH
F32, BF16 = jnp.float32, jnp.bfloat16
MAX_COPIES = 192
EXP_SCALE = 0.125 * math.log2(math.e)


def kernel(
    x_ref, enc_ref, wq_ref, wk_ref, wv_ref, wo_ref, mask_ref, count_ref,
    out_ref, xbuf, rows, masks, enc, wq, wk, wv, wo, kv, kvacc, ones, kmask, vmask, qacc, query, ctx,
    part, tsend, trecv, fsend, frecv, send_sem, recv_sem, local_sem,
):
    p, c = lax.axis_index("prod"), lax.axis_index("cand")
    yh, x = p // 4, lax.rem(p, 4)
    yl, z, k = c // 8, lax.rem(c // 2, 4), lax.rem(c, 2)
    y = yh * 2 + yl
    step = lambda v, d: lax.rem(v + (d + 4), 4)

    def dev(yy, xx, zz, kk):
        return (yy // 2) * 4 + xx, lax.rem(yy, 2) * 8 + zz * 2 + kk

    sib = dev(y, x, z, 1 - k)
    xup, xdn = dev(y, step(x, 1), z, k), dev(y, step(x, -1), z, k)
    yup, ydn = dev(step(y, 1), x, z, k), dev(step(y, -1), x, z, k)
    yfar = dev(step(y, 2), x, z, k)
    ypair = dev(yh * 2 + 1 - yl, x, z, k)
    zup, zdn = dev(y, x, step(z, 1), k), dev(y, x, step(z, -1), k)

    barrier = pltpu.get_barrier_semaphore()
    peers = (sib, xup, xdn, yup, ydn, yfar, zup, zdn)
    for d in peers:
        pl.semaphore_signal(barrier, inc=1, device_id=d, device_id_type=MESH)

    sends = []

    def send(src, there, here, d):
        i = len(sends)
        go = pltpu.make_async_remote_copy(
            src_ref=src, dst_ref=there, send_sem=send_sem.at[i], recv_sem=recv_sem.at[i],
            device_id=d, device_id_type=MESH,
        )
        go.start()
        sends.append(go)
        return pltpu.make_async_remote_copy(
            src_ref=src, dst_ref=here, send_sem=send_sem.at[i], recv_sem=recv_sem.at[i],
            device_id=d, device_id_type=MESH,
        ).wait_recv

    nlocal = [0]

    def local(src, dst):
        i = nlocal[0]
        nlocal[0] += 1
        copy = pltpu.make_async_copy(src, dst, local_sem.at[i])
        copy.start()
        return copy.wait

    load_x = local(x_ref, xbuf)
    loads = [
        local(wk_ref, wk.at[p]), local(wv_ref, wv.at[p]), local(enc_ref, enc.at[c]),
        local(wq_ref, wq.at[x, yh, k, yl]),
        local(wo_ref.at[:, pl.ds(0, 256)], wo.at[0, x, yh, k, yl]),
        local(wo_ref.at[:, pl.ds(256, 256)], wo.at[1, x, yh, k, yl]),
    ]

    flags = mask_ref[...].astype(F32)
    lane = lax.broadcasted_iota(jnp.int32, (8, 256), 1)
    masks[z] = jnp.where(lane < 128, flags[:, 0:1], flags[:, 1:2])

    head = lax.broadcasted_iota(jnp.int32, (256, 256), 1) // 64
    for h in range(4):
        ones[h] = jnp.where(head == h, 1.0, 0.0).astype(BF16)

    load_x()

    def norm_rows(i, carry):
        part_rows = pl.ds(pl.multiple_of(i * 16, 16), 16)
        values = xbuf[part_rows, :].astype(F32)
        scale = lax.rsqrt(jnp.mean(values * values, axis=-1, keepdims=True) + 1e-06)
        rows[z, part_rows, :] = (values * scale).astype(BF16)
        return carry

    lax.fori_loop(0, 8, norm_rows, 0)
    pl.semaphore_wait(barrier, len(peers))

    class Plane:
        def __init__(self, src, buf, x_first, order):
            self.src, self.buf, self.x_first, self.order = src, buf, x_first, order
            self.half = buf.shape[-2] // 2
            self.a, self.b = (x, y) if x_first else (y, x)
            self.aup, self.adn = (xup, xdn) if x_first else (yup, ydn)
            self.bup, self.bdn = (yup, ydn) if x_first else (xup, xdn)
            self.got_b, self.got_far, self.got_sib = {}, {}, {}

        def slot(self, aa, bb, kk):
            yy, xx = (bb, aa) if self.x_first else (aa, bb)
            return self.buf.at[xx, yy // 2, kk, lax.rem(yy, 2)]

        def chunk(self, i, kk):
            aa = self.order[i]
            if self.x_first:
                return self.buf.at[aa, :, kk]
            return self.buf.at[:, aa // 2, kk, lax.rem(aa, 2)]

        def first(self, aa, bb):
            return self.slot(aa, bb, k).at[pl.ds(0, self.half)]

        def second(self, aa, bb):
            return self.slot(aa, bb, k).at[pl.ds(self.half, self.half)]

        def a_start(self):
            here = self.slot(self.a, self.b, k)
            self.got_a = [
                send(self.src, here, self.slot(step(self.a, -1), self.b, k), self.aup),
                send(self.src, here, self.slot(step(self.a, 1), self.b, k), self.adn),
            ]

        def a_forward(self):
            for got in self.got_a:
                got()
            lo, hi, far = (step(self.a, d) for d in (-1, 1, 2))
            self.got_afar = [
                send(self.first(lo, self.b), self.first(lo, self.b), self.first(far, self.b), self.aup),
                send(self.second(hi, self.b), self.second(hi, self.b), self.second(far, self.b), self.adn),
            ]

        def a_finish(self):
            for got in self.got_afar:
                got()

        def b_start(self, i):
            aa = self.order[i]
            here = self.slot(aa, self.b, k)
            src = self.src if i == 0 else here
            self.got_b[i] = [
                send(src, here, self.slot(aa, step(self.b, -1), k), self.bup),
                send(src, here, self.slot(aa, step(self.b, 1), k), self.bdn),
            ]

        def b_forward(self, i):
            aa = self.order[i]
            for got in self.got_b[i]:
                got()
            lo, hi, far = (step(self.b, d) for d in (-1, 1, 2))
            self.got_far[i] = [
                send(self.first(aa, lo), self.first(aa, lo), self.first(aa, far), self.bup),
                send(self.second(aa, hi), self.second(aa, hi), self.second(aa, far), self.bdn),
            ]

        def b_finish(self, i):
            for got in self.got_far[i]:
                got()
            self.got_sib[i] = send(self.chunk(i, k), self.chunk(i, k), self.chunk(i, 1 - k), sib)

        def ready(self, i):
            self.got_sib[i]()

    def kv_ring(src, buf, g):
        here = buf.at[g * 4 + x]
        return [
            send(src, here, buf.at[g * 4 + step(x, -1)], xup),
            send(src, here, buf.at[g * 4 + step(x, 1)], xdn),
        ]

    def kv_forward(buf, g):
        lo, hi, far = (buf.at[g * 4 + step(x, d)] for d in (-1, 1, 2))
        a, b = pl.ds(0, 256), pl.ds(256, 256)
        return [
            send(lo.at[a], lo.at[a], far.at[a], xup),
            send(hi.at[b], hi.at[b], far.at[b], xdn),
        ]

    xs = (x, step(x, -1), step(x, 1), step(x, 2))
    y2 = yh * 2 + 1 - yl
    ys = (y, y2, step(y, 2), step(y2, 2))
    gq = Plane(wq_ref, wq, True, xs)
    ga = Plane(wo_ref.at[:, pl.ds(0, 256)], wo.at[0], True, xs)
    gb = Plane(wo_ref.at[:, pl.ds(256, 256)], wo.at[1], False, ys)

    def slot_e(yy, zz, kk):
        return enc.at[yy * 8 + zz * 2 + kk]

    enc_pair = send(enc_ref, slot_e(yl, z, k), slot_e(1 - yl, z, k), ypair)
    gq.a_start()
    other = 1 - yh
    kv_far = [
        send(wk_ref, wk.at[p], wk.at[other * 4 + x], yfar),
        send(wv_ref, wv.at[p], wv.at[other * 4 + x], yfar),
    ]
    gq.b_start(0)
    kv_own = kv_ring(wk_ref, wk, yh) + kv_ring(wv_ref, wv, yh)
    enc_z = [
        send(enc_ref, slot_e(yl, z, k), slot_e(yl, step(z, -1), k), zup),
        send(enc_ref, slot_e(yl, z, k), slot_e(yl, step(z, 1), k), zdn),
    ]
    mask_z = [
        send(masks.at[z], masks.at[z], masks.at[step(z, -1)], zup),
        send(masks.at[z], masks.at[z], masks.at[step(z, 1)], zdn),
    ]
    rows_z = [
        send(rows.at[z], rows.at[z], rows.at[step(z, -1)], zup),
        send(rows.at[z], rows.at[z], rows.at[step(z, 1)], zdn),
    ]
    enc_sib = [send(enc_ref, slot_e(yl, z, k), slot_e(yl, z, 1 - k), sib)]
    lo, hi, far = step(z, -1), step(z, 1), step(z, 2)

    for wait in loads:
        wait()
    enc_pair()
    enc_sib.append(send(slot_e(1 - yl, z, k), slot_e(1 - yl, z, k), slot_e(1 - yl, z, 1 - k), sib))
    enc_zp = [
        send(slot_e(1 - yl, z, k), slot_e(1 - yl, z, k), slot_e(1 - yl, lo, k), zup),
        send(slot_e(1 - yl, z, k), slot_e(1 - yl, z, k), slot_e(1 - yl, hi, k), zdn),
    ]
    gq.a_forward()
    gq.b_start(1)
    gq.b_start(2)
    for got in kv_far:
        got()
    kv_oth = kv_ring(wk.at[other * 4 + x], wk, other) + kv_ring(wv.at[other * 4 + x], wv, other)
    gq.b_forward(0)
    for got in kv_own:
        got()
    kv_fwd = kv_forward(wk, yh) + kv_forward(wv, yh)
    gq.a_finish()
    gq.b_start(3)

    for got in mask_z:
        got()
    mask_far = send(masks.at[lo], masks.at[lo], masks.at[far], zup)
    for got in enc_z:
        got()
    enc_far = [send(slot_e(yl, lo, k), slot_e(yl, lo, k), slot_e(yl, far, k), zup)]
    for zz in (lo, hi):
        enc_sib.append(send(slot_e(yl, zz, k), slot_e(yl, zz, k), slot_e(yl, zz, 1 - k), sib))
    for got in enc_zp:
        got()
    enc_far.append(send(slot_e(1 - yl, hi, k), slot_e(1 - yl, hi, k), slot_e(1 - yl, far, k), zdn))
    for zz in (lo, hi):
        enc_sib.append(
            send(slot_e(1 - yl, zz, k), slot_e(1 - yl, zz, k), slot_e(1 - yl, zz, 1 - k), sib)
        )
    for got in rows_z:
        got()
    top, low = pl.ds(0, 64), pl.ds(64, 64)
    rows_far = [
        send(rows.at[lo, top], rows.at[lo, top], rows.at[far, top], zup),
        send(rows.at[hi, low], rows.at[hi, low], rows.at[far, low], zdn),
    ]
    gq.b_forward(1)
    for got in kv_oth:
        got()
    kv_last = kv_forward(wk, other) + kv_forward(wv, other)
    ga.a_start()
    gq.b_forward(2)
    for got in enc_far:
        got()
    for yy in (yl, 1 - yl):
        enc_sib.append(send(slot_e(yy, far, k), slot_e(yy, far, k), slot_e(yy, far, 1 - k), sib))

    block, block_sib = k * 2 + yl, (1 - k) * 2 + yl
    pair, pair_sib = k * 2 + 1 - yl, (1 - k) * 2 + 1 - yl

    def project(q, fresh=False):
        lanes = pl.ds(pl.multiple_of(q * 512, 512), 512)
        left = enc[:, :, lanes].reshape(256, 512)
        for i, w in enumerate((wk, wv)):
            term = jnp.dot(left, w[q], preferred_element_type=F32)
            kvacc[i] = term if fresh else kvacc[i] + term

    def add_query(chunks, fresh=False, last=False):
        def tile(blk, carry):
            total = jnp.zeros((512, 256), F32) if fresh else qacc[blk]
            for g, xx in [(g, xx) for xx in chunks for g in range(2)]:
                lanes = pl.ds(pl.multiple_of((g * 4 + xx) * 512, 512), 512)
                total += jnp.dot(
                    rows[:, :, lanes].reshape(512, 512), wq[xx, g, blk // 2, lax.rem(blk, 2)],
                    preferred_element_type=F32,
                )
            if last:
                query[blk] = total.astype(BF16)
            else:
                qacc[blk] = total
            return carry

        lax.fori_loop(0, 4, tile, 0)

    for got in kv_fwd + enc_sib:
        got()
    project(yh * 4 + x, fresh=True)
    for d in (-1, 1, 2):
        project(yh * 4 + step(x, d))
    gq.b_finish(0)
    gq.b_forward(3)
    for d in (0, -1, 1):
        project(other * 4 + step(x, d))
    gq.b_finish(1)
    for got in rows_far:
        got()
    gq.ready(0)
    add_query(xs[:1], fresh=True)
    gq.b_finish(2)
    for got in kv_last:
        got()
    project(other * 4 + step(x, 2))
    kv[block, 0] = kvacc[0].T.astype(BF16)
    kv[block, 1] = kvacc[1].astype(BF16)
    kv_pair = send(kv.at[block], kv.at[block], kv.at[pair], ypair)
    kv_sib = [send(kv.at[block], kv.at[block], kv.at[block_sib], sib)]
    ga.a_forward()
    gb.a_start()
    gq.ready(1)
    gq.ready(2)
    add_query(xs[1:3])
    for i in range(3):
        ga.b_start(i)
    gb.b_start(0)
    gq.b_finish(3)

    def attend(blk):
        keys, values = kv[blk, 0].astype(F32), kv[blk, 1].astype(F32)
        at_row = lax.broadcasted_iota(jnp.int32, (256, 256), 0) // 64
        at_col = lax.broadcasted_iota(jnp.int32, (256, 256), 1) // 64
        num, den = jnp.zeros((512, 256), F32), jnp.zeros((512, 256), F32)
        for h in range(4):
            kmask[h] = jnp.where(at_row == h, keys, 0.0).astype(BF16)
            vmask[h] = jnp.where(at_col == h, values, 0.0).astype(BF16)
            scores = jnp.dot(query[blk], kmask[h], preferred_element_type=F32)
            scores = jnp.where(masks[:, 0:1, :] > 0.5, scores.reshape(4, 128, 256), -1e30)
            best = jnp.max(scores, axis=-1, keepdims=True)
            weights = jnp.exp2((scores - best) * EXP_SCALE).astype(BF16).reshape(512, 256)
            num += jnp.dot(weights, vmask[h], preferred_element_type=F32)
            den += jnp.dot(weights, ones[h], preferred_element_type=F32)
        lanes = pl.ds(pl.multiple_of(blk * 256, 256), 256)
        ctx[:, :, lanes] = (num / den).astype(BF16).reshape(4, 128, 256)

    kv_sib[0]()
    gq.ready(3)
    add_query(xs[3:], last=True)
    gb.a_forward()
    gb.b_start(1)
    gb.b_start(3)
    ga.a_finish()
    ga.b_start(3)
    mask_far()
    attend(block)
    kv_pair()
    kv_sib.append(send(kv.at[pair], kv.at[pair], kv.at[pair_sib], sib))
    ga.b_forward(0)
    gb.b_forward(0)
    attend(block_sib)
    gb.a_finish()
    gb.b_start(2)
    ga.b_forward(1)
    ga.b_forward(2)
    gb.b_forward(1)
    attend(pair)
    ga.b_finish(0)
    gb.b_forward(3)
    ga.b_forward(3)
    kv_sib[1]()
    attend(pair_sib)

    got_t, got_f = {}, {}
    live = (c < count_ref[...]).astype(F32)

    def columns(j, h):
        if j < 4:
            return 0, h * 4 + xs[j]
        g = yh if j < 6 else other
        return 1, g * 4 + xs[(j % 2) * 2 + h]

    def start_sums(j):
        for h in range(2):
            lanes = pl.ds(h * 256, 256)
            side, q = columns(j, h)
            part[j, :, :, lanes] = jnp.dot(
                ctx[...].reshape(512, 1024),
                wo[side, lax.rem(q, 4), q // 4].reshape(1024, 256),
                preferred_element_type=F32,
            ).reshape(4, 128, 256)
        tsend[j, 0] = part[j, far, 0:64].astype(BF16)
        tsend[j, 1] = part[j, far, 64:128].astype(BF16)
        got_t[j] = [
            send(tsend.at[j, 0], trecv.at[j, 0], trecv.at[j, 0], zup),
            send(tsend.at[j, 1], trecv.at[j, 1], trecv.at[j, 1], zdn),
        ]

    def pass_sums(j):
        for got in got_t[j]:
            got()
        fsend[j, 0, 0:64] = (part[j, hi, 0:64] + trecv[j, 0].astype(F32)).astype(BF16)
        fsend[j, 0, 64:128] = part[j, hi, 64:128].astype(BF16)
        fsend[j, 1, 0:64] = part[j, lo, 0:64].astype(BF16)
        fsend[j, 1, 64:128] = (part[j, lo, 64:128] + trecv[j, 1].astype(F32)).astype(BF16)
        got_f[j] = [
            send(fsend.at[j, 0], frecv.at[j, 0], frecv.at[j, 0], zup),
            send(fsend.at[j, 1], frecv.at[j, 1], frecv.at[j, 1], zdn),
        ]

    def end_sums(j):
        for got in got_f[j]:
            got()
        total = part[j, z] + frecv[j, 0].astype(F32) + frecv[j, 1].astype(F32)
        total = (total * live).astype(BF16)
        for h in range(2):
            side, q = columns(j, h)
            lanes = pl.ds(pl.multiple_of(q * 512 + side * 256, 256), 256)
            out_ref[:, lanes] = total[:, h * 256 : (h + 1) * 256]

    ga.b_finish(1)
    ga.b_finish(2)
    ga.ready(0)
    start_sums(0)
    ga.ready(1)
    start_sums(1)
    gb.b_finish(0)
    gb.b_forward(2)
    ga.b_finish(3)
    ga.ready(2)
    start_sums(2)
    gb.b_finish(1)
    gb.b_finish(3)
    pass_sums(0)
    ga.ready(3)
    start_sums(3)
    gb.b_finish(2)
    pass_sums(1)
    gb.ready(0)
    gb.ready(1)
    start_sums(4)
    pass_sums(2)
    start_sums(5)
    pass_sums(3)
    gb.ready(2)
    gb.ready(3)
    start_sums(6)
    pass_sums(4)
    start_sums(7)
    pass_sums(5)
    end_sums(0)
    pass_sums(6)
    end_sums(1)
    pass_sums(7)
    for j in range(2, 8):
        end_sums(j)
    for copy in sends:
        copy.wait_send()


def fused(x, enc, wq, wk, wv, wo, mask, count):
    vmem = pltpu.VMEM
    return pl.pallas_call(
        kernel,
        out_shape=jax.ShapeDtypeStruct((128, 4096), BF16),
        in_specs=[pl.BlockSpec(memory_space=pl.ANY)] * 6
        + [pl.BlockSpec(memory_space=pltpu.VMEM)] * 2,
        out_specs=pl.BlockSpec(memory_space=pltpu.VMEM),
        scratch_shapes=[
            vmem((128, 4096), BF16),
            vmem((4, 128, 4096), BF16),
            vmem((4, 8, 256), F32),
            vmem((16, 16, 4096), BF16),
            vmem((4, 2, 2, 2, 512, 256), BF16),
            vmem((8, 512, 256), BF16),
            vmem((8, 512, 256), BF16),
            vmem((2, 4, 2, 2, 2, 256, 256), BF16),
            vmem((4, 2, 256, 256), BF16),
            vmem((2, 256, 256), F32),
            vmem((4, 256, 256), BF16),
            vmem((4, 256, 256), BF16),
            vmem((4, 256, 256), BF16),
            vmem((4, 512, 256), F32),
            vmem((4, 512, 256), BF16),
            vmem((4, 128, 1024), BF16),
            vmem((8, 4, 128, 512), F32),
            vmem((8, 2, 64, 512), BF16),
            vmem((8, 2, 64, 512), BF16),
            vmem((8, 2, 128, 512), BF16),
            vmem((8, 2, 128, 512), BF16),
            pltpu.SemaphoreType.DMA((MAX_COPIES,)),
            pltpu.SemaphoreType.DMA((MAX_COPIES,)),
            pltpu.SemaphoreType.DMA((8,)),
        ],
        compiler_params=pltpu.CompilerParams(
            collective_id=0, has_side_effects=True, vmem_limit_bytes=60 << 20
        ),
        name="cross_attention",
    )(x, enc, wq, wk, wv, wo, mask, count)


def shards(cand_states, enc_rows, w_query, w_key, w_value, w_out, tile_mask, counts):
    total = fused(
        cand_states[0, 0], enc_rows[0], w_query, w_key, w_value, w_out, tile_mask[0], counts[None]
    )
    return total[None, None]


def solution(mesh):
    return jax.shard_map(
        shards,
        mesh=mesh,
        in_specs=(
            P("prod", "cand", None, None),
            P("prod", "cand", None),
            P("prod", "cand"),
            P("prod", "cand"),
            P("prod", "cand"),
            P("cand", "prod"),
            P("prod", "cand", None),
            P("prod"),
        ),
        out_specs=P("prod", "cand", None, None),
        check_vma=False,
    )
```

```python
import math

import jax
import jax.numpy as jnp
from jax import lax
from jax.experimental import pallas as pl
from jax.experimental.pallas import tpu as pltpu
from jax.sharding import PartitionSpec as P

MESH = pl.DeviceIdType.MESH
F32, BF16 = jnp.float32, jnp.bfloat16
MAX_COPIES = 192
EXP_SCALE = 0.125 * math.log2(math.e)


def kernel(
    x_ref, enc_ref, wq_ref, wk_ref, wv_ref, wo_ref, mask_ref, count_ref,
    out_ref, xbuf, rows, masks, enc, wq, wk, wv, wo, kv, kvacc, ones, kmask, vmask, qacc, query, ctx,
    part, tsend, trecv, fsend, frecv, send_sem, recv_sem, local_sem,
):
    p, c = lax.axis_index("prod"), lax.axis_index("cand")
    yh, x = p // 4, lax.rem(p, 4)
    yl, z, k = c // 8, lax.rem(c // 2, 4), lax.rem(c, 2)
    y = yh * 2 + yl
    step = lambda v, d: lax.rem(v + (d + 4), 4)

    def dev(yy, xx, zz, kk):
        return (yy // 2) * 4 + xx, lax.rem(yy, 2) * 8 + zz * 2 + kk

    sib = dev(y, x, z, 1 - k)
    xup, xdn = dev(y, step(x, 1), z, k), dev(y, step(x, -1), z, k)
    yup, ydn = dev(step(y, 1), x, z, k), dev(step(y, -1), x, z, k)
    yfar = dev(step(y, 2), x, z, k)
    ypair = dev(yh * 2 + 1 - yl, x, z, k)
    zup, zdn = dev(y, x, step(z, 1), k), dev(y, x, step(z, -1), k)

    barrier = pltpu.get_barrier_semaphore()
    peers = (sib, xup, xdn, yup, ydn, yfar, zup, zdn)
    for d in peers:
        pl.semaphore_signal(barrier, inc=1, device_id=d, device_id_type=MESH)

    sends = []

    def send(src, there, here, d):
        i = len(sends)
        go = pltpu.make_async_remote_copy(
            src_ref=src, dst_ref=there, send_sem=send_sem.at[i], recv_sem=recv_sem.at[i],
            device_id=d, device_id_type=MESH,
        )
        go.start()
        sends.append(go)
        return pltpu.make_async_remote_copy(
            src_ref=src, dst_ref=here, send_sem=send_sem.at[i], recv_sem=recv_sem.at[i],
            device_id=d, device_id_type=MESH,
        ).wait_recv

    nlocal = [0]

    def local(src, dst):
        i = nlocal[0]
        nlocal[0] += 1
        copy = pltpu.make_async_copy(src, dst, local_sem.at[i])
        copy.start()
        return copy.wait

    load_x = local(x_ref, xbuf)
    loads = [
        local(wk_ref, wk.at[p]), local(wv_ref, wv.at[p]), local(enc_ref, enc.at[c]),
        local(wq_ref, wq.at[x, yh, k, yl]),
        local(wo_ref.at[:, pl.ds(0, 256)], wo.at[0, x, yh, k, yl]),
        local(wo_ref.at[:, pl.ds(256, 256)], wo.at[1, x, yh, k, yl]),
    ]

    flags = mask_ref[...].astype(F32)
    lane = lax.broadcasted_iota(jnp.int32, (8, 256), 1)
    masks[z] = jnp.where(lane < 128, flags[:, 0:1], flags[:, 1:2])

    head = lax.broadcasted_iota(jnp.int32, (256, 256), 1) // 64
    for h in range(4):
        ones[h] = jnp.where(head == h, 1.0, 0.0).astype(BF16)

    load_x()

    def norm_rows(i, carry):
        part_rows = pl.ds(pl.multiple_of(i * 16, 16), 16)
        values = xbuf[part_rows, :].astype(F32)
        scale = lax.rsqrt(jnp.mean(values * values, axis=-1, keepdims=True) + 1e-06)
        rows[z, part_rows, :] = (values * scale).astype(BF16)
        return carry

    lax.fori_loop(0, 8, norm_rows, 0)
    pl.semaphore_wait(barrier, len(peers))

    class Plane:
        def __init__(self, src, buf, x_first, order):
            self.src, self.buf, self.x_first, self.order = src, buf, x_first, order
            self.half = buf.shape[-2] // 2
            self.a, self.b = (x, y) if x_first else (y, x)
            self.aup, self.adn = (xup, xdn) if x_first else (yup, ydn)
            self.bup, self.bdn = (yup, ydn) if x_first else (xup, xdn)
            self.got_b, self.got_far, self.got_sib = {}, {}, {}

        def slot(self, aa, bb, kk):
            yy, xx = (bb, aa) if self.x_first else (aa, bb)
            return self.buf.at[xx, yy // 2, kk, lax.rem(yy, 2)]

        def chunk(self, i, kk):
            aa = self.order[i]
            if self.x_first:
                return self.buf.at[aa, :, kk]
            return self.buf.at[:, aa // 2, kk, lax.rem(aa, 2)]

        def first(self, aa, bb):
            return self.slot(aa, bb, k).at[pl.ds(0, self.half)]

        def second(self, aa, bb):
            return self.slot(aa, bb, k).at[pl.ds(self.half, self.half)]

        def a_start(self):
            here = self.slot(self.a, self.b, k)
            self.got_a = [
                send(self.src, here, self.slot(step(self.a, -1), self.b, k), self.aup),
                send(self.src, here, self.slot(step(self.a, 1), self.b, k), self.adn),
            ]

        def a_forward(self):
            for got in self.got_a:
                got()
            lo, hi, far = (step(self.a, d) for d in (-1, 1, 2))
            self.got_afar = [
                send(self.first(lo, self.b), self.first(lo, self.b), self.first(far, self.b), self.aup),
                send(self.second(hi, self.b), self.second(hi, self.b), self.second(far, self.b), self.adn),
            ]

        def a_finish(self):
            for got in self.got_afar:
                got()

        def b_start(self, i):
            aa = self.order[i]
            here = self.slot(aa, self.b, k)
            src = self.src if i == 0 else here
            self.got_b[i] = [
                send(src, here, self.slot(aa, step(self.b, -1), k), self.bup),
                send(src, here, self.slot(aa, step(self.b, 1), k), self.bdn),
            ]

        def b_forward(self, i):
            aa = self.order[i]
            for got in self.got_b[i]:
                got()
            lo, hi, far = (step(self.b, d) for d in (-1, 1, 2))
            self.got_far[i] = [
                send(self.first(aa, lo), self.first(aa, lo), self.first(aa, far), self.bup),
                send(self.second(aa, hi), self.second(aa, hi), self.second(aa, far), self.bdn),
            ]

        def b_finish(self, i):
            for got in self.got_far[i]:
                got()
            self.got_sib[i] = send(self.chunk(i, k), self.chunk(i, k), self.chunk(i, 1 - k), sib)

        def ready(self, i):
            self.got_sib[i]()

    def kv_ring(src, buf, g):
        here = buf.at[g * 4 + x]
        return [
            send(src, here, buf.at[g * 4 + step(x, -1)], xup),
            send(src, here, buf.at[g * 4 + step(x, 1)], xdn),
        ]

    def kv_forward(buf, g):
        lo, hi, far = (buf.at[g * 4 + step(x, d)] for d in (-1, 1, 2))
        a, b = pl.ds(0, 256), pl.ds(256, 256)
        return [
            send(lo.at[a], lo.at[a], far.at[a], xup),
            send(hi.at[b], hi.at[b], far.at[b], xdn),
        ]

    xs = (x, step(x, -1), step(x, 1), step(x, 2))
    y2 = yh * 2 + 1 - yl
    ys = (y, y2, step(y, 2), step(y2, 2))
    gq = Plane(wq_ref, wq, True, xs)
    ga = Plane(wo_ref.at[:, pl.ds(0, 256)], wo.at[0], True, xs)
    gb = Plane(wo_ref.at[:, pl.ds(256, 256)], wo.at[1], False, ys)

    def slot_e(yy, zz, kk):
        return enc.at[yy * 8 + zz * 2 + kk]

    enc_pair = send(enc_ref, slot_e(yl, z, k), slot_e(1 - yl, z, k), ypair)
    gq.a_start()
    other = 1 - yh
    kv_far = [
        send(wk_ref, wk.at[p], wk.at[other * 4 + x], yfar),
        send(wv_ref, wv.at[p], wv.at[other * 4 + x], yfar),
    ]
    gq.b_start(0)
    kv_own = kv_ring(wk_ref, wk, yh) + kv_ring(wv_ref, wv, yh)
    enc_z = [
        send(enc_ref, slot_e(yl, z, k), slot_e(yl, step(z, -1), k), zup),
        send(enc_ref, slot_e(yl, z, k), slot_e(yl, step(z, 1), k), zdn),
    ]
    mask_z = [
        send(masks.at[z], masks.at[z], masks.at[step(z, -1)], zup),
        send(masks.at[z], masks.at[z], masks.at[step(z, 1)], zdn),
    ]
    rows_z = [
        send(rows.at[z], rows.at[z], rows.at[step(z, -1)], zup),
        send(rows.at[z], rows.at[z], rows.at[step(z, 1)], zdn),
    ]
    enc_sib = [send(enc_ref, slot_e(yl, z, k), slot_e(yl, z, 1 - k), sib)]
    lo, hi, far = step(z, -1), step(z, 1), step(z, 2)

    for wait in loads:
        wait()
    enc_pair()
    enc_sib.append(send(slot_e(1 - yl, z, k), slot_e(1 - yl, z, k), slot_e(1 - yl, z, 1 - k), sib))
    enc_zp = [
        send(slot_e(1 - yl, z, k), slot_e(1 - yl, z, k), slot_e(1 - yl, lo, k), zup),
        send(slot_e(1 - yl, z, k), slot_e(1 - yl, z, k), slot_e(1 - yl, hi, k), zdn),
    ]
    gq.a_forward()
    gq.b_start(1)
    gq.b_start(2)
    for got in kv_far:
        got()
    kv_oth = kv_ring(wk.at[other * 4 + x], wk, other) + kv_ring(wv.at[other * 4 + x], wv, other)
    gq.b_forward(0)
    for got in kv_own:
        got()
    kv_fwd = kv_forward(wk, yh) + kv_forward(wv, yh)
    gq.a_finish()
    gq.b_start(3)

    for got in mask_z:
        got()
    mask_far = send(masks.at[lo], masks.at[lo], masks.at[far], zup)
    for got in enc_z:
        got()
    enc_far = [send(slot_e(yl, lo, k), slot_e(yl, lo, k), slot_e(yl, far, k), zup)]
    for zz in (lo, hi):
        enc_sib.append(send(slot_e(yl, zz, k), slot_e(yl, zz, k), slot_e(yl, zz, 1 - k), sib))
    gq.b_forward(1)
    for got in enc_zp:
        got()
    enc_far.append(send(slot_e(1 - yl, hi, k), slot_e(1 - yl, hi, k), slot_e(1 - yl, far, k), zdn))
    for zz in (lo, hi):
        enc_sib.append(
            send(slot_e(1 - yl, zz, k), slot_e(1 - yl, zz, k), slot_e(1 - yl, zz, 1 - k), sib)
        )
    for got in rows_z:
        got()
    top, low = pl.ds(0, 64), pl.ds(64, 64)
    rows_far = [
        send(rows.at[lo, top], rows.at[lo, top], rows.at[far, top], zup),
        send(rows.at[hi, low], rows.at[hi, low], rows.at[far, low], zdn),
    ]
    for got in kv_oth:
        got()
    kv_last = kv_forward(wk, other) + kv_forward(wv, other)
    gb.b_start(0)
    ga.a_start()
    gq.b_forward(2)
    for got in enc_far:
        got()
    for yy in (yl, 1 - yl):
        enc_sib.append(send(slot_e(yy, far, k), slot_e(yy, far, k), slot_e(yy, far, 1 - k), sib))

    block, block_sib = k * 2 + yl, (1 - k) * 2 + yl
    pair, pair_sib = k * 2 + 1 - yl, (1 - k) * 2 + 1 - yl

    def project(q, fresh=False):
        lanes = pl.ds(pl.multiple_of(q * 512, 512), 512)
        left = enc[:, :, lanes].reshape(256, 512)
        for i, w in enumerate((wk, wv)):
            term = jnp.dot(left, w[q], preferred_element_type=F32)
            kvacc[i] = term if fresh else kvacc[i] + term

    def add_query(chunks, fresh=False, last=False):
        def tile(blk, carry):
            total = jnp.zeros((512, 256), F32) if fresh else qacc[blk]
            for g, xx in [(g, xx) for xx in chunks for g in range(2)]:
                lanes = pl.ds(pl.multiple_of((g * 4 + xx) * 512, 512), 512)
                total += jnp.dot(
                    rows[:, :, lanes].reshape(512, 512), wq[xx, g, blk // 2, lax.rem(blk, 2)],
                    preferred_element_type=F32,
                )
            if last:
                query[blk] = total.astype(BF16)
            else:
                qacc[blk] = total
            return carry

        lax.fori_loop(0, 4, tile, 0)

    for got in kv_fwd + enc_sib:
        got()
    project(yh * 4 + x, fresh=True)
    for d in (-1, 1, 2):
        project(yh * 4 + step(x, d))
    for d in (0, -1, 1):
        project(other * 4 + step(x, d))
    gq.b_finish(0)
    gq.b_forward(3)
    gb.a_start()
    for got in kv_last:
        got()
    project(other * 4 + step(x, 2))
    kv[block, 0] = kvacc[0].T.astype(BF16)
    kv[block, 1] = kvacc[1].astype(BF16)
    kv_pair = send(kv.at[block], kv.at[block], kv.at[pair], ypair)
    kv_sib = [send(kv.at[block], kv.at[block], kv.at[block_sib], sib)]
    gq.b_finish(1)
    for got in rows_far:
        got()
    gq.ready(0)
    gq.b_finish(2)
    gq.ready(1)
    add_query(xs[:2], fresh=True)
    gq.b_finish(3)
    ga.a_forward()
    ga.b_start(0)
    gb.b_forward(0)
    gb.a_forward()
    gb.b_start(1)
    ga.b_start(1)
    gq.ready(2)
    add_query(xs[2:3])

    def attend(blk):
        keys, values = kv[blk, 0].astype(F32), kv[blk, 1].astype(F32)
        at_row = lax.broadcasted_iota(jnp.int32, (256, 256), 0) // 64
        at_col = lax.broadcasted_iota(jnp.int32, (256, 256), 1) // 64
        num, den = jnp.zeros((512, 256), F32), jnp.zeros((512, 256), F32)
        for h in range(4):
            kmask[h] = jnp.where(at_row == h, keys, 0.0).astype(BF16)
            vmask[h] = jnp.where(at_col == h, values, 0.0).astype(BF16)
            scores = jnp.dot(query[blk], kmask[h], preferred_element_type=F32)
            scores = jnp.where(masks[:, 0:1, :] > 0.5, scores.reshape(4, 128, 256), -1e30)
            best = jnp.max(scores, axis=-1, keepdims=True)
            weights = jnp.exp2((scores - best) * EXP_SCALE).astype(BF16).reshape(512, 256)
            num += jnp.dot(weights, vmask[h], preferred_element_type=F32)
            den += jnp.dot(weights, ones[h], preferred_element_type=F32)
        lanes = pl.ds(pl.multiple_of(blk * 256, 256), 256)
        ctx[:, :, lanes] = (num / den).astype(BF16).reshape(4, 128, 256)

    gq.ready(3)
    add_query(xs[3:], last=True)
    mask_far()
    kv_sib[0]()
    attend(block)
    gb.b_finish(0)
    gb.b_forward(1)
    gb.b_start(3)
    attend(block_sib)
    kv_pair()
    kv_sib.append(send(kv.at[pair], kv.at[pair], kv.at[pair_sib], sib))
    attend(pair)
    gb.b_finish(1)
    kv_sib[1]()
    attend(pair_sib)

    got_t, got_f = {}, {}
    live = (c < count_ref[...]).astype(F32)

    def columns(j, h):
        if j in (2, 3, 6, 7):
            return 0, h * 4 + xs[j % 2 + (j // 4) * 2]
        g = yh if j < 2 else other
        return 1, g * 4 + xs[(j % 2) * 2 + h]

    def start_sums(j):
        for h in range(2):
            lanes = pl.ds(h * 256, 256)
            side, q = columns(j, h)
            part[j, :, :, lanes] = jnp.dot(
                ctx[...].reshape(512, 1024),
                wo[side, lax.rem(q, 4), q // 4].reshape(1024, 256),
                preferred_element_type=F32,
            ).reshape(4, 128, 256)
        tsend[j, 0] = part[j, far, 0:64].astype(BF16)
        tsend[j, 1] = part[j, far, 64:128].astype(BF16)
        got_t[j] = [
            send(tsend.at[j, 0], trecv.at[j, 0], trecv.at[j, 0], zup),
            send(tsend.at[j, 1], trecv.at[j, 1], trecv.at[j, 1], zdn),
        ]

    def pass_sums(j):
        for got in got_t[j]:
            got()
        fsend[j, 0, 0:64] = (part[j, hi, 0:64] + trecv[j, 0].astype(F32)).astype(BF16)
        fsend[j, 0, 64:128] = part[j, hi, 64:128].astype(BF16)
        fsend[j, 1, 0:64] = part[j, lo, 0:64].astype(BF16)
        fsend[j, 1, 64:128] = (part[j, lo, 64:128] + trecv[j, 1].astype(F32)).astype(BF16)
        got_f[j] = [
            send(fsend.at[j, 0], frecv.at[j, 0], frecv.at[j, 0], zup),
            send(fsend.at[j, 1], frecv.at[j, 1], frecv.at[j, 1], zdn),
        ]

    def end_sums(j):
        for got in got_f[j]:
            got()
        total = part[j, z] + frecv[j, 0].astype(F32) + frecv[j, 1].astype(F32)
        total = (total * live).astype(BF16)
        for h in range(2):
            side, q = columns(j, h)
            lanes = pl.ds(pl.multiple_of(q * 512 + side * 256, 256), 256)
            out_ref[:, lanes] = total[:, h * 256 : (h + 1) * 256]

    gb.ready(0)
    gb.ready(1)
    start_sums(0)
    ga.b_forward(0)
    ga.b_start(2)
    start_sums(1)
    gb.b_forward(3)
    gb.a_finish()
    gb.b_start(2)
    pass_sums(0)
    ga.b_finish(0)
    ga.b_forward(1)
    ga.a_finish()
    ga.b_start(3)
    pass_sums(1)
    ga.ready(0)
    start_sums(2)
    ga.b_finish(1)
    gb.b_finish(3)
    gb.b_forward(2)
    ga.b_forward(2)
    ga.ready(1)
    start_sums(3)
    pass_sums(2)
    ga.b_forward(3)
    gb.b_finish(2)
    ga.b_finish(2)
    pass_sums(3)
    gb.ready(2)
    gb.ready(3)
    start_sums(4)
    start_sums(5)
    ga.b_finish(3)
    ga.ready(2)
    start_sums(6)
    pass_sums(4)
    ga.ready(3)
    start_sums(7)
    pass_sums(5)
    end_sums(0)
    pass_sums(6)
    end_sums(1)
    pass_sums(7)
    for j in range(2, 8):
        end_sums(j)
    for copy in sends:
        copy.wait_send()


def fused(x, enc, wq, wk, wv, wo, mask, count):
    vmem = pltpu.VMEM
    return pl.pallas_call(
        kernel,
        out_shape=jax.ShapeDtypeStruct((128, 4096), BF16),
        in_specs=[pl.BlockSpec(memory_space=pl.ANY)] * 6
        + [pl.BlockSpec(memory_space=pltpu.VMEM)] * 2,
        out_specs=pl.BlockSpec(memory_space=pltpu.VMEM),
        scratch_shapes=[
            vmem((128, 4096), BF16),
            vmem((4, 128, 4096), BF16),
            vmem((4, 8, 256), F32),
            vmem((16, 16, 4096), BF16),
            vmem((4, 2, 2, 2, 512, 256), BF16),
            vmem((8, 512, 256), BF16),
            vmem((8, 512, 256), BF16),
            vmem((2, 4, 2, 2, 2, 256, 256), BF16),
            vmem((4, 2, 256, 256), BF16),
            vmem((2, 256, 256), F32),
            vmem((4, 256, 256), BF16),
            vmem((4, 256, 256), BF16),
            vmem((4, 256, 256), BF16),
            vmem((4, 512, 256), F32),
            vmem((4, 512, 256), BF16),
            vmem((4, 128, 1024), BF16),
            vmem((8, 4, 128, 512), F32),
            vmem((8, 2, 64, 512), BF16),
            vmem((8, 2, 64, 512), BF16),
            vmem((8, 2, 128, 512), BF16),
            vmem((8, 2, 128, 512), BF16),
            pltpu.SemaphoreType.DMA((MAX_COPIES,)),
            pltpu.SemaphoreType.DMA((MAX_COPIES,)),
            pltpu.SemaphoreType.DMA((8,)),
        ],
        compiler_params=pltpu.CompilerParams(
            collective_id=0, has_side_effects=True, vmem_limit_bytes=60 << 20
        ),
        name="cross_attention",
    )(x, enc, wq, wk, wv, wo, mask, count)


def shards(cand_states, enc_rows, w_query, w_key, w_value, w_out, tile_mask, counts):
    total = fused(
        cand_states[0, 0], enc_rows[0], w_query, w_key, w_value, w_out, tile_mask[0], counts[None]
    )
    return total[None, None]


def solution(mesh):
    return jax.shard_map(
        shards,
        mesh=mesh,
        in_specs=(
            P("prod", "cand", None, None),
            P("prod", "cand", None),
            P("prod", "cand"),
            P("prod", "cand"),
            P("prod", "cand"),
            P("cand", "prod"),
            P("prod", "cand", None),
            P("prod"),
        ),
        out_specs=P("prod", "cand", None, None),
        check_vma=False,
    )
```

```python
import math

import jax
import jax.numpy as jnp
from jax import lax
from jax.experimental import pallas as pl
from jax.experimental.pallas import tpu as pltpu
from jax.sharding import PartitionSpec as P

MESH = pl.DeviceIdType.MESH
F32, BF16 = jnp.float32, jnp.bfloat16
MAX_COPIES = 192
EXP_SCALE = 0.125 * math.log2(math.e)


def kernel(
    x_ref, enc_ref, wq_ref, wk_ref, wv_ref, wo_ref, mask_ref, count_ref,
    out_ref, xbuf, rows, masks, enc, wq, wk, wv, wo, kv, kvacc, kmask, vmask, qacc, query, ctx,
    part, tsend, trecv, fsend, frecv, send_sem, recv_sem, local_sem,
):
    p, c = lax.axis_index("prod"), lax.axis_index("cand")
    yh, x = p // 4, lax.rem(p, 4)
    yl, z, k = c // 8, lax.rem(c // 2, 4), lax.rem(c, 2)
    y = yh * 2 + yl
    step = lambda v, d: lax.rem(v + (d + 4), 4)

    def dev(yy, xx, zz, kk):
        return (yy // 2) * 4 + xx, lax.rem(yy, 2) * 8 + zz * 2 + kk

    sib = dev(y, x, z, 1 - k)
    xup, xdn = dev(y, step(x, 1), z, k), dev(y, step(x, -1), z, k)
    yup, ydn = dev(step(y, 1), x, z, k), dev(step(y, -1), x, z, k)
    yfar = dev(step(y, 2), x, z, k)
    ypair = dev(yh * 2 + 1 - yl, x, z, k)
    zup, zdn = dev(y, x, step(z, 1), k), dev(y, x, step(z, -1), k)

    barrier = pltpu.get_barrier_semaphore()
    peers = (sib, xup, xdn, yup, ydn, yfar, zup, zdn)
    for d in peers:
        pl.semaphore_signal(barrier, inc=1, device_id=d, device_id_type=MESH)

    sends = []

    def send(src, there, here, d):
        i = len(sends)
        go = pltpu.make_async_remote_copy(
            src_ref=src, dst_ref=there, send_sem=send_sem.at[i], recv_sem=recv_sem.at[i],
            device_id=d, device_id_type=MESH,
        )
        go.start()
        sends.append(go)
        return pltpu.make_async_remote_copy(
            src_ref=src, dst_ref=here, send_sem=send_sem.at[i], recv_sem=recv_sem.at[i],
            device_id=d, device_id_type=MESH,
        ).wait_recv

    nlocal = [0]

    def local(src, dst):
        i = nlocal[0]
        nlocal[0] += 1
        copy = pltpu.make_async_copy(src, dst, local_sem.at[i])
        copy.start()
        return copy.wait

    load_x = local(x_ref, xbuf)
    loads = [
        local(wk_ref, wk.at[p]), local(wv_ref, wv.at[p]), local(enc_ref, enc.at[c]),
        local(wq_ref, wq.at[x, yh, k, yl]),
        local(wo_ref.at[:, pl.ds(0, 256)], wo.at[0, x, yh, k, yl]),
        local(wo_ref.at[:, pl.ds(256, 256)], wo.at[1, x, yh, k, yl]),
    ]

    flags = mask_ref[...].astype(F32)
    lane = lax.broadcasted_iota(jnp.int32, (8, 256), 1)
    masks[z] = jnp.where(lane < 128, flags[:, 0:1], flags[:, 1:2])

    pl.semaphore_wait(barrier, len(peers))

    class Plane:
        def __init__(self, src, buf, x_first, order):
            self.src, self.buf, self.x_first, self.order = src, buf, x_first, order
            self.half = buf.shape[-2] // 2
            self.a, self.b = (x, y) if x_first else (y, x)
            self.aup, self.adn = (xup, xdn) if x_first else (yup, ydn)
            self.bup, self.bdn = (yup, ydn) if x_first else (xup, xdn)
            self.got_b, self.got_far, self.got_sib = {}, {}, {}

        def slot(self, aa, bb, kk):
            yy, xx = (bb, aa) if self.x_first else (aa, bb)
            return self.buf.at[xx, yy // 2, kk, lax.rem(yy, 2)]

        def chunk(self, i, kk):
            aa = self.order[i]
            if self.x_first:
                return self.buf.at[aa, :, kk]
            return self.buf.at[:, aa // 2, kk, lax.rem(aa, 2)]

        def first(self, aa, bb):
            return self.slot(aa, bb, k).at[pl.ds(0, self.half)]

        def second(self, aa, bb):
            return self.slot(aa, bb, k).at[pl.ds(self.half, self.half)]

        def a_start(self):
            here = self.slot(self.a, self.b, k)
            self.got_a = [
                send(self.src, here, self.slot(step(self.a, -1), self.b, k), self.aup),
                send(self.src, here, self.slot(step(self.a, 1), self.b, k), self.adn),
            ]

        def a_forward(self):
            for got in self.got_a:
                got()
            lo, hi, far = (step(self.a, d) for d in (-1, 1, 2))
            self.got_afar = [
                send(self.first(lo, self.b), self.first(lo, self.b), self.first(far, self.b), self.aup),
                send(self.second(hi, self.b), self.second(hi, self.b), self.second(far, self.b), self.adn),
            ]

        def a_finish(self):
            for got in self.got_afar:
                got()

        def b_start(self, i):
            aa = self.order[i]
            here = self.slot(aa, self.b, k)
            src = self.src if i == 0 else here
            self.got_b[i] = [
                send(src, here, self.slot(aa, step(self.b, -1), k), self.bup),
                send(src, here, self.slot(aa, step(self.b, 1), k), self.bdn),
            ]

        def b_forward(self, i):
            aa = self.order[i]
            for got in self.got_b[i]:
                got()
            lo, hi, far = (step(self.b, d) for d in (-1, 1, 2))
            self.got_far[i] = [
                send(self.first(aa, lo), self.first(aa, lo), self.first(aa, far), self.bup),
                send(self.second(aa, hi), self.second(aa, hi), self.second(aa, far), self.bdn),
            ]

        def b_finish(self, i):
            for got in self.got_far[i]:
                got()
            self.got_sib[i] = send(self.chunk(i, k), self.chunk(i, k), self.chunk(i, 1 - k), sib)

        def ready(self, i):
            self.got_sib[i]()

    def kv_ring(src, buf, g):
        here = buf.at[g * 4 + x]
        return [
            send(src, here, buf.at[g * 4 + step(x, -1)], xup),
            send(src, here, buf.at[g * 4 + step(x, 1)], xdn),
        ]

    def kv_forward(buf, g):
        lo, hi, far = (buf.at[g * 4 + step(x, d)] for d in (-1, 1, 2))
        a, b = pl.ds(0, 256), pl.ds(256, 256)
        return [
            send(lo.at[a], lo.at[a], far.at[a], xup),
            send(hi.at[b], hi.at[b], far.at[b], xdn),
        ]

    xs = (x, step(x, -1), step(x, 1), step(x, 2))
    y2 = yh * 2 + 1 - yl
    ys = (y, y2, step(y, 2), step(y2, 2))
    gq = Plane(wq_ref, wq, True, xs)
    ga = Plane(wo_ref.at[:, pl.ds(0, 256)], wo.at[0], True, xs)
    gb = Plane(wo_ref.at[:, pl.ds(256, 256)], wo.at[1], False, ys)

    def slot_e(yy, zz, kk):
        return enc.at[yy * 8 + zz * 2 + kk]

    enc_pair = send(enc_ref, slot_e(yl, z, k), slot_e(1 - yl, z, k), ypair)
    gq.a_start()
    other = 1 - yh
    kv_far = [
        send(wk_ref, wk.at[p], wk.at[other * 4 + x], yfar),
        send(wv_ref, wv.at[p], wv.at[other * 4 + x], yfar),
    ]
    gq.b_start(0)
    kv_own = kv_ring(wk_ref, wk, yh) + kv_ring(wv_ref, wv, yh)
    enc_z = [
        send(enc_ref, slot_e(yl, z, k), slot_e(yl, step(z, -1), k), zup),
        send(enc_ref, slot_e(yl, z, k), slot_e(yl, step(z, 1), k), zdn),
    ]
    mask_z = [
        send(masks.at[z], masks.at[z], masks.at[step(z, -1)], zup),
        send(masks.at[z], masks.at[z], masks.at[step(z, 1)], zdn),
    ]
    load_x()

    def norm_rows(i, carry):
        part_rows = pl.ds(pl.multiple_of(i * 16, 16), 16)
        values = xbuf[part_rows, :].astype(F32)
        scale = lax.rsqrt(jnp.mean(values * values, axis=-1, keepdims=True) + 1e-06)
        rows[z, part_rows, :] = (values * scale).astype(BF16)
        return carry

    lax.fori_loop(0, 8, norm_rows, 0)
    rows_z = [
        send(rows.at[z], rows.at[z], rows.at[step(z, -1)], zup),
        send(rows.at[z], rows.at[z], rows.at[step(z, 1)], zdn),
    ]
    enc_sib = [send(enc_ref, slot_e(yl, z, k), slot_e(yl, z, 1 - k), sib)]
    lo, hi, far = step(z, -1), step(z, 1), step(z, 2)

    for wait in loads:
        wait()
    enc_pair()
    enc_sib.append(send(slot_e(1 - yl, z, k), slot_e(1 - yl, z, k), slot_e(1 - yl, z, 1 - k), sib))
    enc_zp = [
        send(slot_e(1 - yl, z, k), slot_e(1 - yl, z, k), slot_e(1 - yl, lo, k), zup),
        send(slot_e(1 - yl, z, k), slot_e(1 - yl, z, k), slot_e(1 - yl, hi, k), zdn),
    ]
    gq.a_forward()
    gq.b_start(1)
    gq.b_start(2)
    for got in kv_far:
        got()
    kv_oth = kv_ring(wk.at[other * 4 + x], wk, other) + kv_ring(wv.at[other * 4 + x], wv, other)
    gq.b_forward(0)
    for got in kv_own:
        got()
    kv_fwd = kv_forward(wk, yh) + kv_forward(wv, yh)
    gq.a_finish()
    gq.b_start(3)

    for got in mask_z:
        got()
    mask_far = send(masks.at[lo], masks.at[lo], masks.at[far], zup)
    for got in enc_z:
        got()
    enc_far = [send(slot_e(yl, lo, k), slot_e(yl, lo, k), slot_e(yl, far, k), zup)]
    for zz in (lo, hi):
        enc_sib.append(send(slot_e(yl, zz, k), slot_e(yl, zz, k), slot_e(yl, zz, 1 - k), sib))
    gq.b_forward(1)
    for got in enc_zp:
        got()
    enc_far.append(send(slot_e(1 - yl, hi, k), slot_e(1 - yl, hi, k), slot_e(1 - yl, far, k), zdn))
    for zz in (lo, hi):
        enc_sib.append(
            send(slot_e(1 - yl, zz, k), slot_e(1 - yl, zz, k), slot_e(1 - yl, zz, 1 - k), sib)
        )
    for got in rows_z:
        got()
    top, low = pl.ds(0, 64), pl.ds(64, 64)
    rows_far = [
        send(rows.at[lo, top], rows.at[lo, top], rows.at[far, top], zup),
        send(rows.at[hi, low], rows.at[hi, low], rows.at[far, low], zdn),
    ]
    for got in kv_oth:
        got()
    kv_last = kv_forward(wk, other) + kv_forward(wv, other)
    gb.b_start(0)
    ga.a_start()
    gq.b_forward(2)
    for got in enc_far:
        got()
    for yy in (yl, 1 - yl):
        enc_sib.append(send(slot_e(yy, far, k), slot_e(yy, far, k), slot_e(yy, far, 1 - k), sib))

    block, block_sib = k * 2 + yl, (1 - k) * 2 + yl
    pair, pair_sib = k * 2 + 1 - yl, (1 - k) * 2 + 1 - yl

    def project(q, fresh=False):
        lanes = pl.ds(pl.multiple_of(q * 512, 512), 512)
        left = enc[:, :, lanes].reshape(256, 512)
        for i, w in enumerate((wk, wv)):
            term = jnp.dot(left, w[q], preferred_element_type=F32)
            kvacc[i] = term if fresh else kvacc[i] + term

    def add_query(xx, fresh=False, last=False):
        for blk in range(4):
            total = jnp.zeros((512, 256), F32) if fresh else qacc[blk]
            for g in range(2):
                lanes = pl.ds(pl.multiple_of((g * 4 + xx) * 512, 512), 512)
                total += jnp.dot(
                    rows[:, :, lanes].reshape(512, 512), wq[xx, g, blk // 2, blk % 2],
                    preferred_element_type=F32,
                )
            if last:
                query[blk] = total.astype(BF16)
            else:
                qacc[blk] = total

    for got in kv_fwd + enc_sib:
        got()
    project(yh * 4 + x, fresh=True)
    for d in (-1, 1, 2):
        project(yh * 4 + step(x, d))
    for d in (0, -1, 1):
        project(other * 4 + step(x, d))
    gq.b_finish(0)
    gq.b_forward(3)
    gb.a_start()
    gq.b_finish(1)
    for got in rows_far:
        got()
    gq.ready(0)
    add_query(xs[0], fresh=True)
    gq.b_finish(2)
    for got in kv_last:
        got()
    project(other * 4 + step(x, 2))
    kv[block, 0] = kvacc[0].T.astype(BF16)
    kv[block, 1] = kvacc[1].astype(BF16)
    kv_pair = send(kv.at[block], kv.at[block], kv.at[pair], ypair)
    kv_sib = [send(kv.at[block], kv.at[block], kv.at[block_sib], sib)]
    gq.ready(1)
    gq.b_finish(3)
    add_query(xs[1])
    gb.b_forward(0)
    gq.ready(2)
    gb.a_forward()
    gb.b_start(1)
    ga.a_forward()
    ga.b_start(0)
    ga.b_start(1)
    add_query(xs[2])

    def attend(blk):
        keys, values = kv[blk, 0].astype(F32), kv[blk, 1].astype(F32)
        at_row = lax.broadcasted_iota(jnp.int32, (256, 256), 0) // 64
        at_col = lax.broadcasted_iota(jnp.int32, (256, 256), 1) // 64
        sums = [jnp.zeros((512, 256), F32) for _ in range(2)]
        for h in range(4):
            kmask[h] = jnp.where(at_row == h, keys, 0.0).astype(BF16)
            one = jnp.where(at_col == (h + 2) % 4, 1.0, 0.0)
            vmask[h] = jnp.where(at_col == h, values, one).astype(BF16)
            scores = jnp.dot(query[blk], kmask[h], preferred_element_type=F32)
            scores = jnp.where(masks[:, 0:1, :] > 0.5, scores.reshape(4, 128, 256), -1e30)
            best = jnp.max(scores, axis=-1, keepdims=True)
            weights = jnp.exp2((scores - best) * EXP_SCALE).astype(BF16).reshape(512, 256)
            sums[h // 2] += jnp.dot(weights, vmask[h], preferred_element_type=F32)
        near = sums[0][:, :128] / sums[0][:, 128:]
        away = sums[1][:, 128:] / sums[1][:, :128]
        lanes = pl.ds(pl.multiple_of(blk * 256, 256), 256)
        ctx[:, :, lanes] = jnp.concatenate([near, away], axis=1).astype(BF16).reshape(4, 128, 256)

    gq.ready(3)
    add_query(xs[3], last=True)
    mask_far()
    kv_sib[0]()
    attend(block)
    gb.b_forward(1)
    gb.b_start(3)
    gb.b_finish(0)
    attend(block_sib)
    kv_pair()
    kv_sib.append(send(kv.at[pair], kv.at[pair], kv.at[pair_sib], sib))
    gb.b_finish(1)
    attend(pair)
    kv_sib[1]()
    attend(pair_sib)
    ga.b_forward(0)
    ga.b_start(2)

    got_t, got_f = {}, {}
    live = (c < count_ref[...]).astype(F32)

    def columns(j, h):
        if j in (2, 3, 6, 7):
            return 0, h * 4 + xs[j % 2 + (j // 4) * 2]
        g = yh if j < 2 else other
        return 1, g * 4 + xs[(j % 2) * 2 + h]

    def start_sums(j):
        for h in range(2):
            lanes = pl.ds(h * 256, 256)
            side, q = columns(j, h)
            part[j, :, :, lanes] = jnp.dot(
                ctx[...].reshape(512, 1024),
                wo[side, lax.rem(q, 4), q // 4].reshape(1024, 256),
                preferred_element_type=F32,
            ).reshape(4, 128, 256)
        tsend[j, 0] = part[j, far, 0:64].astype(BF16)
        tsend[j, 1] = part[j, far, 64:128].astype(BF16)
        got_t[j] = [
            send(tsend.at[j, 0], trecv.at[j, 0], trecv.at[j, 0], zup),
            send(tsend.at[j, 1], trecv.at[j, 1], trecv.at[j, 1], zdn),
        ]

    def pass_sums(j):
        for got in got_t[j]:
            got()
        fsend[j, 0, 0:64] = (part[j, hi, 0:64] + trecv[j, 0].astype(F32)).astype(BF16)
        fsend[j, 0, 64:128] = part[j, hi, 64:128].astype(BF16)
        fsend[j, 1, 0:64] = part[j, lo, 0:64].astype(BF16)
        fsend[j, 1, 64:128] = (part[j, lo, 64:128] + trecv[j, 1].astype(F32)).astype(BF16)
        got_f[j] = [
            send(fsend.at[j, 0], frecv.at[j, 0], frecv.at[j, 0], zup),
            send(fsend.at[j, 1], frecv.at[j, 1], frecv.at[j, 1], zdn),
        ]

    def end_sums(j):
        for got in got_f[j]:
            got()
        total = part[j, z] + frecv[j, 0].astype(F32) + frecv[j, 1].astype(F32)
        total = (total * live).astype(BF16)
        for h in range(2):
            side, q = columns(j, h)
            lanes = pl.ds(pl.multiple_of(q * 512 + side * 256, 256), 256)
            out_ref[:, lanes] = total[:, h * 256 : (h + 1) * 256]

    gb.ready(0)
    gb.ready(1)
    start_sums(0)
    start_sums(1)
    gb.b_forward(3)
    ga.b_finish(0)
    ga.b_forward(1)
    gb.a_finish()
    gb.b_start(2)
    ga.a_finish()
    ga.b_start(3)
    pass_sums(0)
    ga.ready(0)
    start_sums(2)
    pass_sums(1)
    ga.b_finish(1)
    gb.b_finish(3)
    gb.b_forward(2)
    ga.b_forward(2)
    ga.ready(1)
    start_sums(3)
    pass_sums(2)
    ga.b_forward(3)
    gb.b_finish(2)
    ga.b_finish(2)
    gb.ready(2)
    gb.ready(3)
    start_sums(4)
    pass_sums(3)
    start_sums(5)
    ga.b_finish(3)
    pass_sums(4)
    ga.ready(2)
    start_sums(6)
    pass_sums(5)
    ga.ready(3)
    start_sums(7)
    pass_sums(6)
    end_sums(0)
    end_sums(1)
    pass_sums(7)
    for j in range(2, 8):
        end_sums(j)
    for copy in sends:
        copy.wait_send()


def fused(x, enc, wq, wk, wv, wo, mask, count):
    vmem = pltpu.VMEM
    return pl.pallas_call(
        kernel,
        out_shape=jax.ShapeDtypeStruct((128, 4096), BF16),
        in_specs=[pl.BlockSpec(memory_space=pl.ANY)] * 6
        + [pl.BlockSpec(memory_space=pltpu.VMEM)] * 2,
        out_specs=pl.BlockSpec(memory_space=pltpu.VMEM),
        scratch_shapes=[
            vmem((128, 4096), BF16),
            vmem((4, 128, 4096), BF16),
            vmem((4, 8, 256), F32),
            vmem((16, 16, 4096), BF16),
            vmem((4, 2, 2, 2, 512, 256), BF16),
            vmem((8, 512, 256), BF16),
            vmem((8, 512, 256), BF16),
            vmem((2, 4, 2, 2, 2, 256, 256), BF16),
            vmem((4, 2, 256, 256), BF16),
            vmem((2, 256, 256), F32),
            vmem((4, 256, 256), BF16),
            vmem((4, 256, 256), BF16),
            vmem((4, 512, 256), F32),
            vmem((4, 512, 256), BF16),
            vmem((4, 128, 1024), BF16),
            vmem((8, 4, 128, 512), F32),
            vmem((8, 2, 64, 512), BF16),
            vmem((8, 2, 64, 512), BF16),
            vmem((8, 2, 128, 512), BF16),
            vmem((8, 2, 128, 512), BF16),
            pltpu.SemaphoreType.DMA((MAX_COPIES,)),
            pltpu.SemaphoreType.DMA((MAX_COPIES,)),
            pltpu.SemaphoreType.DMA((8,)),
        ],
        compiler_params=pltpu.CompilerParams(
            collective_id=0, has_side_effects=True, vmem_limit_bytes=60 << 20
        ),
        name="cross_attention",
    )(x, enc, wq, wk, wv, wo, mask, count)


def shards(cand_states, enc_rows, w_query, w_key, w_value, w_out, tile_mask, counts):
    total = fused(
        cand_states[0, 0], enc_rows[0], w_query, w_key, w_value, w_out, tile_mask[0], counts[None]
    )
    return total[None, None]


def solution(mesh):
    return jax.shard_map(
        shards,
        mesh=mesh,
        in_specs=(
            P("prod", "cand", None, None),
            P("prod", "cand", None),
            P("prod", "cand"),
            P("prod", "cand"),
            P("prod", "cand"),
            P("cand", "prod"),
            P("prod", "cand", None),
            P("prod"),
        ),
        out_specs=P("prod", "cand", None, None),
        check_vma=False,
    )
```

```python
import math

import jax
import jax.numpy as jnp
from jax import lax
from jax.experimental import pallas as pl
from jax.experimental.pallas import tpu as pltpu
from jax.sharding import PartitionSpec as P

MESH = pl.DeviceIdType.MESH
F32, BF16 = jnp.float32, jnp.bfloat16
MAX_COPIES = 192
EXP_SCALE = 0.125 * math.log2(math.e)


def kernel(
    x_ref, enc_ref, wq_ref, wk_ref, wv_ref, wo_ref, mask_ref, count_ref,
    out_ref, xbuf, rows, masks, enc, wq, wk, wv, wo_a, wo_b, kv, kvacc, kmask, vmask, qacc, query, ctx,
    part, tsend, trecv, fsend, frecv, send_sem, recv_sem, local_sem,
):
    p, c = lax.axis_index("prod"), lax.axis_index("cand")
    yh, x = p // 4, lax.rem(p, 4)
    yl, z, k = c // 8, lax.rem(c // 2, 4), lax.rem(c, 2)
    y = yh * 2 + yl
    step = lambda v, d: lax.rem(v + (d + 4), 4)

    def dev(yy, xx, zz, kk):
        return (yy // 2) * 4 + xx, lax.rem(yy, 2) * 8 + zz * 2 + kk

    sib = dev(y, x, z, 1 - k)
    xup, xdn = dev(y, step(x, 1), z, k), dev(y, step(x, -1), z, k)
    yup, ydn = dev(step(y, 1), x, z, k), dev(step(y, -1), x, z, k)
    yfar = dev(step(y, 2), x, z, k)
    ypair = dev(yh * 2 + 1 - yl, x, z, k)
    zup, zdn = dev(y, x, step(z, 1), k), dev(y, x, step(z, -1), k)

    barrier = pltpu.get_barrier_semaphore()
    peers = (sib, xup, xdn, yup, ydn, yfar, zup, zdn)
    for d in peers:
        pl.semaphore_signal(barrier, inc=1, device_id=d, device_id_type=MESH)

    sends = []

    def send(src, there, here, d):
        i = len(sends)
        go = pltpu.make_async_remote_copy(
            src_ref=src, dst_ref=there, send_sem=send_sem.at[i], recv_sem=recv_sem.at[i],
            device_id=d, device_id_type=MESH,
        )
        go.start()
        sends.append(go)
        return pltpu.make_async_remote_copy(
            src_ref=src, dst_ref=here, send_sem=send_sem.at[i], recv_sem=recv_sem.at[i],
            device_id=d, device_id_type=MESH,
        ).wait_recv

    nlocal = [0]

    def local(src, dst):
        i = nlocal[0]
        nlocal[0] += 1
        copy = pltpu.make_async_copy(src, dst, local_sem.at[i])
        copy.start()
        return copy.wait

    load_x = local(x_ref, xbuf)
    loads = [
        local(wk_ref, wk.at[p]), local(wv_ref, wv.at[p]), local(enc_ref, enc.at[c]),
        local(wq_ref, wq.at[x, yh, k, yl]),
        local(wo_ref.at[:, pl.ds(0, 128)], wo_a.at[x, yh, k, yl]),
        local(wo_ref.at[:, pl.ds(128, 384)], wo_b.at[x, yh, k, yl]),
    ]

    flags = mask_ref[...].astype(F32)
    lane = lax.broadcasted_iota(jnp.int32, (8, 256), 1)
    masks[z] = jnp.where(lane < 128, flags[:, 0:1], flags[:, 1:2])

    pl.semaphore_wait(barrier, len(peers))

    class Plane:
        def __init__(self, src, buf, x_first, order):
            self.src, self.buf, self.x_first, self.order = src, buf, x_first, order
            self.half = buf.shape[-2] // 2
            self.a, self.b = (x, y) if x_first else (y, x)
            self.aup, self.adn = (xup, xdn) if x_first else (yup, ydn)
            self.bup, self.bdn = (yup, ydn) if x_first else (xup, xdn)
            self.got_b, self.got_far, self.got_sib = {}, {}, {}

        def slot(self, aa, bb, kk):
            yy, xx = (bb, aa) if self.x_first else (aa, bb)
            return self.buf.at[xx, yy // 2, kk, lax.rem(yy, 2)]

        def chunk(self, i, kk):
            aa = self.order[i]
            if self.x_first:
                return self.buf.at[aa, :, kk]
            return self.buf.at[:, aa // 2, kk, lax.rem(aa, 2)]

        def first(self, aa, bb):
            return self.slot(aa, bb, k).at[pl.ds(0, self.half)]

        def second(self, aa, bb):
            return self.slot(aa, bb, k).at[pl.ds(self.half, self.half)]

        def a_start(self):
            here = self.slot(self.a, self.b, k)
            self.got_a = [
                send(self.src, here, self.slot(step(self.a, -1), self.b, k), self.aup),
                send(self.src, here, self.slot(step(self.a, 1), self.b, k), self.adn),
            ]

        def a_forward(self):
            for got in self.got_a:
                got()
            lo, hi, far = (step(self.a, d) for d in (-1, 1, 2))
            self.got_afar = [
                send(self.first(lo, self.b), self.first(lo, self.b), self.first(far, self.b), self.aup),
                send(self.second(hi, self.b), self.second(hi, self.b), self.second(far, self.b), self.adn),
            ]

        def a_finish(self):
            for got in self.got_afar:
                got()

        def b_start(self, i):
            aa = self.order[i]
            here = self.slot(aa, self.b, k)
            src = self.src if i == 0 else here
            self.got_b[i] = [
                send(src, here, self.slot(aa, step(self.b, -1), k), self.bup),
                send(src, here, self.slot(aa, step(self.b, 1), k), self.bdn),
            ]

        def b_forward(self, i):
            aa = self.order[i]
            for got in self.got_b[i]:
                got()
            lo, hi, far = (step(self.b, d) for d in (-1, 1, 2))
            self.got_far[i] = [
                send(self.first(aa, lo), self.first(aa, lo), self.first(aa, far), self.bup),
                send(self.second(aa, hi), self.second(aa, hi), self.second(aa, far), self.bdn),
            ]

        def b_finish(self, i):
            for got in self.got_far[i]:
                got()
            self.got_sib[i] = send(self.chunk(i, k), self.chunk(i, k), self.chunk(i, 1 - k), sib)

        def ready(self, i):
            self.got_sib[i]()

    def kv_ring(src, buf, g):
        here = buf.at[g * 4 + x]
        return [
            send(src, here, buf.at[g * 4 + step(x, -1)], xup),
            send(src, here, buf.at[g * 4 + step(x, 1)], xdn),
        ]

    def kv_forward(buf, g):
        lo, hi, far = (buf.at[g * 4 + step(x, d)] for d in (-1, 1, 2))
        a, b = pl.ds(0, 256), pl.ds(256, 256)
        return [
            send(lo.at[a], lo.at[a], far.at[a], xup),
            send(hi.at[b], hi.at[b], far.at[b], xdn),
        ]

    xs = (x, step(x, -1), step(x, 1), step(x, 2))
    y2 = yh * 2 + 1 - yl
    ys = (y, y2, step(y, 2), step(y2, 2))
    gq = Plane(wq_ref, wq, True, xs)
    ga = Plane(wo_ref.at[:, pl.ds(0, 128)], wo_a, True, xs)
    gb = Plane(wo_ref.at[:, pl.ds(128, 384)], wo_b, False, ys)

    def slot_e(yy, zz, kk):
        return enc.at[yy * 8 + zz * 2 + kk]

    enc_pair = send(enc_ref, slot_e(yl, z, k), slot_e(1 - yl, z, k), ypair)
    gq.a_start()
    other = 1 - yh
    kv_far = [
        send(wk_ref, wk.at[p], wk.at[other * 4 + x], yfar),
        send(wv_ref, wv.at[p], wv.at[other * 4 + x], yfar),
    ]
    gq.b_start(0)
    kv_own = kv_ring(wk_ref, wk, yh) + kv_ring(wv_ref, wv, yh)
    enc_z = [
        send(enc_ref, slot_e(yl, z, k), slot_e(yl, step(z, -1), k), zup),
        send(enc_ref, slot_e(yl, z, k), slot_e(yl, step(z, 1), k), zdn),
    ]
    mask_z = [
        send(masks.at[z], masks.at[z], masks.at[step(z, -1)], zup),
        send(masks.at[z], masks.at[z], masks.at[step(z, 1)], zdn),
    ]
    load_x()

    def norm_rows(i, carry):
        part_rows = pl.ds(pl.multiple_of(i * 16, 16), 16)
        values = xbuf[part_rows, :].astype(F32)
        scale = lax.rsqrt(jnp.mean(values * values, axis=-1, keepdims=True) + 1e-06)
        rows[z, part_rows, :] = (values * scale).astype(BF16)
        return carry

    lax.fori_loop(0, 8, norm_rows, 0)
    rows_z = [
        send(rows.at[z], rows.at[z], rows.at[step(z, -1)], zup),
        send(rows.at[z], rows.at[z], rows.at[step(z, 1)], zdn),
    ]
    enc_sib = [send(enc_ref, slot_e(yl, z, k), slot_e(yl, z, 1 - k), sib)]
    lo, hi, far = step(z, -1), step(z, 1), step(z, 2)

    for wait in loads:
        wait()
    enc_pair()
    enc_sib.append(send(slot_e(1 - yl, z, k), slot_e(1 - yl, z, k), slot_e(1 - yl, z, 1 - k), sib))
    enc_zp = [
        send(slot_e(1 - yl, z, k), slot_e(1 - yl, z, k), slot_e(1 - yl, lo, k), zup),
        send(slot_e(1 - yl, z, k), slot_e(1 - yl, z, k), slot_e(1 - yl, hi, k), zdn),
    ]
    gq.a_forward()
    gq.b_start(1)
    gq.b_start(2)
    for got in kv_far:
        got()
    kv_oth = kv_ring(wk.at[other * 4 + x], wk, other) + kv_ring(wv.at[other * 4 + x], wv, other)
    gq.b_forward(0)
    for got in kv_own:
        got()
    kv_fwd = kv_forward(wk, yh) + kv_forward(wv, yh)
    gq.a_finish()
    gq.b_start(3)

    for got in mask_z:
        got()
    mask_far = send(masks.at[lo], masks.at[lo], masks.at[far], zup)
    for got in enc_z:
        got()
    enc_far = [send(slot_e(yl, lo, k), slot_e(yl, lo, k), slot_e(yl, far, k), zup)]
    for zz in (lo, hi):
        enc_sib.append(send(slot_e(yl, zz, k), slot_e(yl, zz, k), slot_e(yl, zz, 1 - k), sib))
    gq.b_forward(1)
    for got in enc_zp:
        got()
    enc_far.append(send(slot_e(1 - yl, hi, k), slot_e(1 - yl, hi, k), slot_e(1 - yl, far, k), zdn))
    for zz in (lo, hi):
        enc_sib.append(
            send(slot_e(1 - yl, zz, k), slot_e(1 - yl, zz, k), slot_e(1 - yl, zz, 1 - k), sib)
        )
    for got in rows_z:
        got()
    top, low = pl.ds(0, 64), pl.ds(64, 64)
    rows_far = [
        send(rows.at[lo, top], rows.at[lo, top], rows.at[far, top], zup),
        send(rows.at[hi, low], rows.at[hi, low], rows.at[far, low], zdn),
    ]
    for got in kv_oth:
        got()
    kv_last = kv_forward(wk, other) + kv_forward(wv, other)
    gb.b_start(0)
    ga.a_start()
    gq.b_forward(2)
    for got in enc_far:
        got()
    for yy in (yl, 1 - yl):
        enc_sib.append(send(slot_e(yy, far, k), slot_e(yy, far, k), slot_e(yy, far, 1 - k), sib))

    block, block_sib = k * 2 + yl, (1 - k) * 2 + yl
    pair, pair_sib = k * 2 + 1 - yl, (1 - k) * 2 + 1 - yl

    def project(q, fresh=False):
        lanes = pl.ds(pl.multiple_of(q * 512, 512), 512)
        left = enc[:, :, lanes].reshape(256, 512)
        for i, w in enumerate((wk, wv)):
            term = jnp.dot(left, w[q], preferred_element_type=F32)
            kvacc[i] = term if fresh else kvacc[i] + term

    def add_query(xx, fresh=False, last=False):
        for blk in range(4):
            total = jnp.zeros((512, 256), F32) if fresh else qacc[blk]
            for g in range(2):
                lanes = pl.ds(pl.multiple_of((g * 4 + xx) * 512, 512), 512)
                total += jnp.dot(
                    rows[:, :, lanes].reshape(512, 512), wq[xx, g, blk // 2, blk % 2],
                    preferred_element_type=F32,
                )
            if last:
                query[blk] = total.astype(BF16)
            else:
                qacc[blk] = total

    for got in kv_fwd + enc_sib:
        got()
    project(yh * 4 + x, fresh=True)
    for d in (-1, 1, 2):
        project(yh * 4 + step(x, d))
    for d in (0, -1, 1):
        project(other * 4 + step(x, d))
    gb.a_start()
    gq.b_finish(0)
    gq.b_forward(3)
    gq.b_finish(1)
    for got in rows_far:
        got()
    gq.ready(0)
    add_query(xs[0], fresh=True)
    gq.b_finish(2)
    for got in kv_last:
        got()
    project(other * 4 + step(x, 2))
    kv[block, 0] = kvacc[0].T.astype(BF16)
    kv[block, 1] = kvacc[1].astype(BF16)
    kv_pair = send(kv.at[block], kv.at[block], kv.at[pair], ypair)
    kv_sib = [send(kv.at[block], kv.at[block], kv.at[block_sib], sib)]
    gq.ready(1)
    add_query(xs[1])
    gb.b_forward(0)
    gb.a_forward()
    gb.b_start(1)
    gq.b_finish(3)
    ga.a_forward()
    ga.b_start(0)
    ga.b_start(1)
    gq.ready(2)
    add_query(xs[2])
    gb.b_forward(1)
    gb.b_start(3)

    def attend(blk):
        keys, values = kv[blk, 0].astype(F32), kv[blk, 1].astype(F32)
        at_row = lax.broadcasted_iota(jnp.int32, (256, 256), 0) // 64
        at_col = lax.broadcasted_iota(jnp.int32, (256, 256), 1) // 64
        sums = [jnp.zeros((512, 256), F32) for _ in range(2)]
        for h in range(4):
            kmask[h] = jnp.where(at_row == h, keys, 0.0).astype(BF16)
            one = jnp.where(at_col == (h + 2) % 4, 1.0, 0.0)
            vmask[h] = jnp.where(at_col == h, values, one).astype(BF16)
            scores = jnp.dot(query[blk], kmask[h], preferred_element_type=F32)
            scores = jnp.where(masks[:, 0:1, :] > 0.5, scores.reshape(4, 128, 256), -1e30)
            best = jnp.max(scores, axis=-1, keepdims=True)
            weights = jnp.exp2((scores - best) * EXP_SCALE).astype(BF16).reshape(512, 256)
            sums[h // 2] += jnp.dot(weights, vmask[h], preferred_element_type=F32)
        near = sums[0][:, :128] / sums[0][:, 128:]
        away = sums[1][:, 128:] / sums[1][:, :128]
        lanes = pl.ds(pl.multiple_of(blk * 256, 256), 256)
        ctx[:, :, lanes] = jnp.concatenate([near, away], axis=1).astype(BF16).reshape(4, 128, 256)

    gq.ready(3)
    add_query(xs[3], last=True)
    mask_far()
    kv_sib[0]()
    attend(block)
    gb.b_finish(0)
    gb.b_finish(1)
    attend(block_sib)
    kv_pair()
    kv_sib.append(send(kv.at[pair], kv.at[pair], kv.at[pair_sib], sib))
    attend(pair)
    kv_sib[1]()
    attend(pair_sib)
    ga.b_forward(0)
    ga.b_start(2)

    got_t, got_f = {}, {}
    live = (c < count_ref[...]).astype(F32)

    def columns(j, h):
        if j in (3, 4):
            xx = xs[(j - 3) * 2 + h]
            return [(wo_a, xx, g, 0, 128, (g * 4 + xx) * 512) for g in range(2)]
        g, m = (yh, j) if j < 3 else (other, j - 5)
        if m < 2:
            xx = xs[m * 2 + h]
            return [(wo_b, xx, g, 0, 256, (g * 4 + xx) * 512 + 128)]
        return [(wo_b, xx, g, 256, 128, (g * 4 + xx) * 512 + 384) for xx in xs[h * 2 : h * 2 + 2]]

    def start_sums(j):
        for h in range(2):
            lanes = pl.ds(h * 256, 256)
            right = [
                buf[xx, g, :, :, :, lane : lane + width].reshape(1024, width)
                for buf, xx, g, lane, width, _ in columns(j, h)
            ]
            part[j, :, :, lanes] = jnp.dot(
                ctx[...].reshape(512, 1024),
                right[0] if len(right) == 1 else jnp.concatenate(right, axis=1),
                preferred_element_type=F32,
            ).reshape(4, 128, 256)
        tsend[j, 0] = part[j, far, 0:64].astype(BF16)
        tsend[j, 1] = part[j, far, 64:128].astype(BF16)
        got_t[j] = [
            send(tsend.at[j, 0], trecv.at[j, 0], trecv.at[j, 0], zup),
            send(tsend.at[j, 1], trecv.at[j, 1], trecv.at[j, 1], zdn),
        ]

    def pass_sums(j):
        for got in got_t[j]:
            got()
        fsend[j, 0, 0:64] = (part[j, hi, 0:64] + trecv[j, 0].astype(F32)).astype(BF16)
        fsend[j, 0, 64:128] = part[j, hi, 64:128].astype(BF16)
        fsend[j, 1, 0:64] = part[j, lo, 0:64].astype(BF16)
        fsend[j, 1, 64:128] = (part[j, lo, 64:128] + trecv[j, 1].astype(F32)).astype(BF16)
        got_f[j] = [
            send(fsend.at[j, 0], frecv.at[j, 0], frecv.at[j, 0], zup),
            send(fsend.at[j, 1], frecv.at[j, 1], frecv.at[j, 1], zdn),
        ]

    def end_sums(j):
        for got in got_f[j]:
            got()
        total = part[j, z] + frecv[j, 0].astype(F32) + frecv[j, 1].astype(F32)
        total = (total * live).astype(BF16)
        for h in range(2):
            start = h * 256
            for _, _, _, _, width, column in columns(j, h):
                lanes = pl.ds(pl.multiple_of(column, 128), width)
                out_ref[:, lanes] = total[:, start : start + width]
                start += width

    gb.ready(0)
    gb.ready(1)
    start_sums(0)
    gb.b_forward(3)
    gb.a_finish()
    gb.b_start(2)
    ga.b_forward(1)
    ga.a_finish()
    ga.b_start(3)
    start_sums(1)
    pass_sums(0)
    ga.b_finish(0)
    ga.b_finish(1)
    start_sums(2)
    pass_sums(1)
    ga.b_forward(2)
    gb.b_finish(3)
    gb.b_forward(2)
    ga.ready(0)
    ga.ready(1)
    start_sums(3)
    pass_sums(2)
    ga.b_forward(3)
    ga.b_finish(2)
    ga.b_finish(3)
    gb.b_finish(2)
    ga.ready(2)
    ga.ready(3)
    start_sums(4)
    pass_sums(3)
    gb.ready(2)
    gb.ready(3)
    start_sums(5)
    pass_sums(4)
    start_sums(6)
    pass_sums(5)
    start_sums(7)
    pass_sums(6)
    end_sums(0)
    end_sums(1)
    pass_sums(7)
    for j in range(2, 8):
        end_sums(j)
    for copy in sends:
        copy.wait_send()


def fused(x, enc, wq, wk, wv, wo, mask, count):
    vmem = pltpu.VMEM
    return pl.pallas_call(
        kernel,
        out_shape=jax.ShapeDtypeStruct((128, 4096), BF16),
        in_specs=[pl.BlockSpec(memory_space=pl.ANY)] * 6
        + [pl.BlockSpec(memory_space=pltpu.VMEM)] * 2,
        out_specs=pl.BlockSpec(memory_space=pltpu.VMEM),
        scratch_shapes=[
            vmem((128, 4096), BF16),
            vmem((4, 128, 4096), BF16),
            vmem((4, 8, 256), F32),
            vmem((16, 16, 4096), BF16),
            vmem((4, 2, 2, 2, 512, 256), BF16),
            vmem((8, 512, 256), BF16),
            vmem((8, 512, 256), BF16),
            vmem((4, 2, 2, 2, 256, 128), BF16),
            vmem((4, 2, 2, 2, 256, 384), BF16),
            vmem((4, 2, 256, 256), BF16),
            vmem((2, 256, 256), F32),
            vmem((4, 256, 256), BF16),
            vmem((4, 256, 256), BF16),
            vmem((4, 512, 256), F32),
            vmem((4, 512, 256), BF16),
            vmem((4, 128, 1024), BF16),
            vmem((8, 4, 128, 512), F32),
            vmem((8, 2, 64, 512), BF16),
            vmem((8, 2, 64, 512), BF16),
            vmem((8, 2, 128, 512), BF16),
            vmem((8, 2, 128, 512), BF16),
            pltpu.SemaphoreType.DMA((MAX_COPIES,)),
            pltpu.SemaphoreType.DMA((MAX_COPIES,)),
            pltpu.SemaphoreType.DMA((8,)),
        ],
        compiler_params=pltpu.CompilerParams(
            collective_id=0, has_side_effects=True, vmem_limit_bytes=60 << 20
        ),
        name="cross_attention",
    )(x, enc, wq, wk, wv, wo, mask, count)


def shards(cand_states, enc_rows, w_query, w_key, w_value, w_out, tile_mask, counts):
    total = fused(
        cand_states[0, 0], enc_rows[0], w_query, w_key, w_value, w_out, tile_mask[0], counts[None]
    )
    return total[None, None]


def solution(mesh):
    return jax.shard_map(
        shards,
        mesh=mesh,
        in_specs=(
            P("prod", "cand", None, None),
            P("prod", "cand", None),
            P("prod", "cand"),
            P("prod", "cand"),
            P("prod", "cand"),
            P("cand", "prod"),
            P("prod", "cand", None),
            P("prod"),
        ),
        out_specs=P("prod", "cand", None, None),
        check_vma=False,
    )
```

```python
import math

import jax
import jax.numpy as jnp
from jax import lax
from jax.experimental import pallas as pl
from jax.experimental.pallas import tpu as pltpu
from jax.sharding import PartitionSpec as P

MESH = pl.DeviceIdType.MESH
F32, BF16 = jnp.float32, jnp.bfloat16
MAX_COPIES = 192
EXP_SCALE = 0.125 * math.log2(math.e)


def kernel(
    x_ref, enc_ref, wq_ref, wk_ref, wv_ref, wo_ref, mask_ref, count_ref,
    out_ref, xbuf, rows, masks, enc, wq, wk, wv, wo, kv, kvacc, kmask, vmask, qacc, query, ctx,
    part, tsend, trecv, fsend, frecv, send_sem, recv_sem, local_sem,
):
    p, c = lax.axis_index("prod"), lax.axis_index("cand")
    yh, x = p // 4, lax.rem(p, 4)
    yl, z, k = c // 8, lax.rem(c // 2, 4), lax.rem(c, 2)
    y = yh * 2 + yl
    step = lambda v, d: lax.rem(v + (d + 4), 4)

    def dev(yy, xx, zz, kk):
        return (yy // 2) * 4 + xx, lax.rem(yy, 2) * 8 + zz * 2 + kk

    sib = dev(y, x, z, 1 - k)
    xup, xdn = dev(y, step(x, 1), z, k), dev(y, step(x, -1), z, k)
    yup, ydn = dev(step(y, 1), x, z, k), dev(step(y, -1), x, z, k)
    yfar = dev(step(y, 2), x, z, k)
    ypair = dev(yh * 2 + 1 - yl, x, z, k)
    zup, zdn = dev(y, x, step(z, 1), k), dev(y, x, step(z, -1), k)

    barrier = pltpu.get_barrier_semaphore()
    peers = (sib, xup, xdn, yup, ydn, yfar, zup, zdn)
    for d in peers:
        pl.semaphore_signal(barrier, inc=1, device_id=d, device_id_type=MESH)

    sends = []

    def send(src, there, here, d):
        i = len(sends)
        go = pltpu.make_async_remote_copy(
            src_ref=src, dst_ref=there, send_sem=send_sem.at[i], recv_sem=recv_sem.at[i],
            device_id=d, device_id_type=MESH,
        )
        go.start()
        sends.append(go)
        return pltpu.make_async_remote_copy(
            src_ref=src, dst_ref=here, send_sem=send_sem.at[i], recv_sem=recv_sem.at[i],
            device_id=d, device_id_type=MESH,
        ).wait_recv

    nlocal = [0]

    def local(src, dst):
        i = nlocal[0]
        nlocal[0] += 1
        copy = pltpu.make_async_copy(src, dst, local_sem.at[i])
        copy.start()
        return copy.wait

    load_x = local(x_ref, xbuf)
    loads = [
        local(wk_ref, wk.at[p]), local(wv_ref, wv.at[p]), local(enc_ref, enc.at[c]),
        local(wq_ref, wq.at[x, yh, k, yl]),
        local(wo_ref.at[:, pl.ds(0, 256)], wo.at[0, x, yh, k, yl]),
        local(wo_ref.at[:, pl.ds(256, 256)], wo.at[1, x, yh, k, yl]),
    ]

    flags = mask_ref[...].astype(F32)
    lane = lax.broadcasted_iota(jnp.int32, (8, 256), 1)
    masks[z] = jnp.where(lane < 128, flags[:, 0:1], flags[:, 1:2])

    pl.semaphore_wait(barrier, len(peers))

    class Plane:
        def __init__(self, src, buf, x_first, order):
            self.src, self.buf, self.x_first, self.order = src, buf, x_first, order
            self.half = buf.shape[-2] // 2
            self.a, self.b = (x, y) if x_first else (y, x)
            self.aup, self.adn = (xup, xdn) if x_first else (yup, ydn)
            self.bup, self.bdn = (yup, ydn) if x_first else (xup, xdn)
            self.got_b, self.got_far, self.got_sib = {}, {}, {}

        def slot(self, aa, bb, kk):
            yy, xx = (bb, aa) if self.x_first else (aa, bb)
            return self.buf.at[xx, yy // 2, kk, lax.rem(yy, 2)]

        def chunk(self, i, kk):
            aa = self.order[i]
            if self.x_first:
                return self.buf.at[aa, :, kk]
            return self.buf.at[:, aa // 2, kk, lax.rem(aa, 2)]

        def first(self, aa, bb):
            return self.slot(aa, bb, k).at[pl.ds(0, self.half)]

        def second(self, aa, bb):
            return self.slot(aa, bb, k).at[pl.ds(self.half, self.half)]

        def a_start(self):
            here = self.slot(self.a, self.b, k)
            self.got_a = [
                send(self.src, here, self.slot(step(self.a, -1), self.b, k), self.aup),
                send(self.src, here, self.slot(step(self.a, 1), self.b, k), self.adn),
            ]

        def a_forward(self):
            for got in self.got_a:
                got()
            lo, hi, far = (step(self.a, d) for d in (-1, 1, 2))
            self.got_afar = [
                send(self.first(lo, self.b), self.first(lo, self.b), self.first(far, self.b), self.aup),
                send(self.second(hi, self.b), self.second(hi, self.b), self.second(far, self.b), self.adn),
            ]

        def a_finish(self):
            for got in self.got_afar:
                got()

        def b_start(self, i):
            aa = self.order[i]
            here = self.slot(aa, self.b, k)
            src = self.src if i == 0 else here
            self.got_b[i] = [
                send(src, here, self.slot(aa, step(self.b, -1), k), self.bup),
                send(src, here, self.slot(aa, step(self.b, 1), k), self.bdn),
            ]

        def b_forward(self, i):
            aa = self.order[i]
            for got in self.got_b[i]:
                got()
            lo, hi, far = (step(self.b, d) for d in (-1, 1, 2))
            self.got_far[i] = [
                send(self.first(aa, lo), self.first(aa, lo), self.first(aa, far), self.bup),
                send(self.second(aa, hi), self.second(aa, hi), self.second(aa, far), self.bdn),
            ]

        def b_finish(self, i):
            for got in self.got_far[i]:
                got()
            self.got_sib[i] = send(self.chunk(i, k), self.chunk(i, k), self.chunk(i, 1 - k), sib)

        def ready(self, i):
            self.got_sib[i]()

    def kv_ring(src, buf, g):
        here = buf.at[g * 4 + x]
        return [
            send(src, here, buf.at[g * 4 + step(x, -1)], xup),
            send(src, here, buf.at[g * 4 + step(x, 1)], xdn),
        ]

    def kv_forward(buf, g):
        lo, hi, far = (buf.at[g * 4 + step(x, d)] for d in (-1, 1, 2))
        a, b = pl.ds(0, 256), pl.ds(256, 256)
        return [
            send(lo.at[a], lo.at[a], far.at[a], xup),
            send(hi.at[b], hi.at[b], far.at[b], xdn),
        ]

    xs = (x, step(x, -1), step(x, 1), step(x, 2))
    y2 = yh * 2 + 1 - yl
    ys = (y, y2, step(y, 2), step(y2, 2))
    gq = Plane(wq_ref, wq, True, xs)
    ga = Plane(wo_ref.at[:, pl.ds(0, 256)], wo.at[0], True, xs)
    gb = Plane(wo_ref.at[:, pl.ds(256, 256)], wo.at[1], False, ys)

    def slot_e(yy, zz, kk):
        return enc.at[yy * 8 + zz * 2 + kk]

    enc_pair = send(enc_ref, slot_e(yl, z, k), slot_e(1 - yl, z, k), ypair)
    gq.a_start()
    other = 1 - yh
    kv_far = [
        send(wk_ref, wk.at[p], wk.at[other * 4 + x], yfar),
        send(wv_ref, wv.at[p], wv.at[other * 4 + x], yfar),
    ]
    gq.b_start(0)
    kv_own = kv_ring(wk_ref, wk, yh) + kv_ring(wv_ref, wv, yh)
    enc_z = [
        send(enc_ref, slot_e(yl, z, k), slot_e(yl, step(z, -1), k), zup),
        send(enc_ref, slot_e(yl, z, k), slot_e(yl, step(z, 1), k), zdn),
    ]
    mask_z = [
        send(masks.at[z], masks.at[z], masks.at[step(z, -1)], zup),
        send(masks.at[z], masks.at[z], masks.at[step(z, 1)], zdn),
    ]
    load_x()

    def norm_rows(i, carry):
        part_rows = pl.ds(pl.multiple_of(i * 16, 16), 16)
        values = xbuf[part_rows, :].astype(F32)
        scale = lax.rsqrt(jnp.mean(values * values, axis=-1, keepdims=True) + 1e-06)
        rows[z, part_rows, :] = (values * scale).astype(BF16)
        return carry

    lax.fori_loop(0, 8, norm_rows, 0)
    rows_z = [
        send(rows.at[z], rows.at[z], rows.at[step(z, -1)], zup),
        send(rows.at[z], rows.at[z], rows.at[step(z, 1)], zdn),
    ]
    enc_sib = [send(enc_ref, slot_e(yl, z, k), slot_e(yl, z, 1 - k), sib)]
    lo, hi, far = step(z, -1), step(z, 1), step(z, 2)

    for wait in loads:
        wait()
    enc_pair()
    enc_sib.append(send(slot_e(1 - yl, z, k), slot_e(1 - yl, z, k), slot_e(1 - yl, z, 1 - k), sib))
    enc_zp = [
        send(slot_e(1 - yl, z, k), slot_e(1 - yl, z, k), slot_e(1 - yl, lo, k), zup),
        send(slot_e(1 - yl, z, k), slot_e(1 - yl, z, k), slot_e(1 - yl, hi, k), zdn),
    ]
    gq.a_forward()
    gq.b_start(1)
    gq.b_start(2)
    for got in kv_far:
        got()
    kv_oth = kv_ring(wk.at[other * 4 + x], wk, other) + kv_ring(wv.at[other * 4 + x], wv, other)
    gq.b_forward(0)
    for got in kv_own:
        got()
    kv_fwd = kv_forward(wk, yh) + kv_forward(wv, yh)
    gq.a_finish()
    gq.b_start(3)

    for got in mask_z:
        got()
    mask_far = send(masks.at[lo], masks.at[lo], masks.at[far], zup)
    for got in enc_z:
        got()
    enc_far = [send(slot_e(yl, lo, k), slot_e(yl, lo, k), slot_e(yl, far, k), zup)]
    for zz in (lo, hi):
        enc_sib.append(send(slot_e(yl, zz, k), slot_e(yl, zz, k), slot_e(yl, zz, 1 - k), sib))
    gq.b_forward(1)
    for got in enc_zp:
        got()
    enc_far.append(send(slot_e(1 - yl, hi, k), slot_e(1 - yl, hi, k), slot_e(1 - yl, far, k), zdn))
    for zz in (lo, hi):
        enc_sib.append(
            send(slot_e(1 - yl, zz, k), slot_e(1 - yl, zz, k), slot_e(1 - yl, zz, 1 - k), sib)
        )
    for got in rows_z:
        got()
    top, low = pl.ds(0, 64), pl.ds(64, 64)
    rows_far = [
        send(rows.at[lo, top], rows.at[lo, top], rows.at[far, top], zup),
        send(rows.at[hi, low], rows.at[hi, low], rows.at[far, low], zdn),
    ]
    for got in kv_oth:
        got()
    kv_last = kv_forward(wk, other) + kv_forward(wv, other)
    gb.b_start(0)
    ga.a_start()
    gq.b_forward(2)
    for got in enc_far:
        got()
    for yy in (yl, 1 - yl):
        enc_sib.append(send(slot_e(yy, far, k), slot_e(yy, far, k), slot_e(yy, far, 1 - k), sib))

    block, block_sib = k * 2 + yl, (1 - k) * 2 + yl
    pair, pair_sib = k * 2 + 1 - yl, (1 - k) * 2 + 1 - yl

    def project(q, fresh=False):
        lanes = pl.ds(pl.multiple_of(q * 512, 512), 512)
        left = enc[:, :, lanes].reshape(256, 512)
        for i, w in enumerate((wk, wv)):
            term = jnp.dot(left, w[q], preferred_element_type=F32)
            kvacc[i] = term if fresh else kvacc[i] + term

    def add_query(xx, fresh=False, last=False):
        for blk in range(4):
            total = jnp.zeros((512, 256), F32) if fresh else qacc[blk]
            for g in range(2):
                lanes = pl.ds(pl.multiple_of((g * 4 + xx) * 512, 512), 512)
                total += jnp.dot(
                    rows[:, :, lanes].reshape(512, 512), wq[xx, g, blk // 2, blk % 2],
                    preferred_element_type=F32,
                )
            if last:
                query[blk] = total.astype(BF16)
            else:
                qacc[blk] = total

    for got in kv_fwd + enc_sib:
        got()
    project(yh * 4 + x, fresh=True)
    for d in (-1, 1, 2):
        project(yh * 4 + step(x, d))
    for d in (0, -1, 1):
        project(other * 4 + step(x, d))
    gq.b_finish(0)
    gq.b_forward(3)
    gb.a_start()
    gq.b_finish(1)
    for got in rows_far:
        got()
    gq.ready(0)
    add_query(xs[0], fresh=True)
    gq.b_finish(2)
    for got in kv_last:
        got()
    project(other * 4 + step(x, 2))
    kv[block, 0] = kvacc[0].T.astype(BF16)
    kv[block, 1] = kvacc[1].astype(BF16)
    kv_pair = send(kv.at[block], kv.at[block], kv.at[pair], ypair)
    kv_sib = [send(kv.at[block], kv.at[block], kv.at[block_sib], sib)]
    gq.ready(1)
    gq.b_finish(3)
    add_query(xs[1])
    gb.b_forward(0)
    gq.ready(2)
    gb.a_forward()
    gb.b_start(1)
    ga.a_forward()
    ga.b_start(0)
    ga.b_start(1)
    add_query(xs[2])

    def attend(blk):
        keys, values = kv[blk, 0].astype(F32), kv[blk, 1].astype(F32)
        at_row = lax.broadcasted_iota(jnp.int32, (256, 256), 0) // 64
        at_col = lax.broadcasted_iota(jnp.int32, (256, 256), 1) // 64
        sums = [jnp.zeros((512, 256), F32) for _ in range(2)]
        for h in range(4):
            kmask[h] = jnp.where(at_row == h, keys, 0.0).astype(BF16)
            one = jnp.where(at_col == (h + 2) % 4, 1.0, 0.0)
            vmask[h] = jnp.where(at_col == h, values, one).astype(BF16)
            scores = jnp.dot(query[blk], kmask[h], preferred_element_type=F32)
            scores = jnp.where(masks[:, 0:1, :] > 0.5, scores.reshape(4, 128, 256), -1e30)
            best = jnp.max(scores, axis=-1, keepdims=True)
            weights = jnp.exp2((scores - best) * EXP_SCALE).astype(BF16).reshape(512, 256)
            sums[h // 2] += jnp.dot(weights, vmask[h], preferred_element_type=F32)
        near = sums[0][:, :128] / sums[0][:, 128:]
        away = sums[1][:, 128:] / sums[1][:, :128]
        lanes = pl.ds(pl.multiple_of(blk * 256, 256), 256)
        ctx[:, :, lanes] = jnp.concatenate([near, away], axis=1).astype(BF16).reshape(4, 128, 256)

    gq.ready(3)
    add_query(xs[3], last=True)
    mask_far()
    kv_sib[0]()
    attend(block)
    gb.b_forward(1)
    gb.b_start(3)
    gb.b_finish(0)
    attend(block_sib)
    kv_pair()
    kv_sib.append(send(kv.at[pair], kv.at[pair], kv.at[pair_sib], sib))
    gb.b_finish(1)
    attend(pair)
    kv_sib[1]()
    attend(pair_sib)
    ga.b_forward(0)
    ga.b_start(2)

    got_t, got_f = {}, {}
    live = (c < count_ref[...]).astype(F32)

    def columns(j, h):
        if j in (2, 3, 6, 7):
            return 0, h * 4 + xs[j % 2 + (j // 4) * 2]
        g = yh if j < 2 else other
        return 1, g * 4 + xs[(j % 2) * 2 + h]

    def start_sums(j):
        for h in range(2):
            lanes = pl.ds(h * 256, 256)
            side, q = columns(j, h)
            part[j, :, :, lanes] = jnp.dot(
                ctx[...].reshape(512, 1024),
                wo[side, lax.rem(q, 4), q // 4].reshape(1024, 256),
                preferred_element_type=F32,
            ).reshape(4, 128, 256)
        tsend[j, 0] = part[j, far, 0:64].astype(BF16)
        tsend[j, 1] = part[j, far, 64:128].astype(BF16)
        fsend[j, 0, 64:128] = part[j, hi, 64:128].astype(BF16)
        fsend[j, 1, 0:64] = part[j, lo, 0:64].astype(BF16)
        got_t[j] = [
            send(tsend.at[j, 0], trecv.at[j, 0], trecv.at[j, 0], zup),
            send(tsend.at[j, 1], trecv.at[j, 1], trecv.at[j, 1], zdn),
        ]
        got_f[j] = [
            send(fsend.at[j, 0, low], frecv.at[j, 0, low], frecv.at[j, 0, low], zup),
            send(fsend.at[j, 1, top], frecv.at[j, 1, top], frecv.at[j, 1, top], zdn),
        ]

    def pass_sums(j):
        for got in got_t[j]:
            got()
        fsend[j, 0, 0:64] = (part[j, hi, 0:64] + trecv[j, 0].astype(F32)).astype(BF16)
        fsend[j, 1, 64:128] = (part[j, lo, 64:128] + trecv[j, 1].astype(F32)).astype(BF16)
        got_f[j] += [
            send(fsend.at[j, 0, top], frecv.at[j, 0, top], frecv.at[j, 0, top], zup),
            send(fsend.at[j, 1, low], frecv.at[j, 1, low], frecv.at[j, 1, low], zdn),
        ]

    def end_sums(j):
        for got in got_f[j]:
            got()
        total = part[j, z] + frecv[j, 0].astype(F32) + frecv[j, 1].astype(F32)
        total = (total * live).astype(BF16)
        for h in range(2):
            side, q = columns(j, h)
            lanes = pl.ds(pl.multiple_of(q * 512 + side * 256, 256), 256)
            out_ref[:, lanes] = total[:, h * 256 : (h + 1) * 256]

    gb.ready(0)
    gb.ready(1)
    start_sums(0)
    start_sums(1)
    gb.b_forward(3)
    ga.b_finish(0)
    ga.b_forward(1)
    gb.a_finish()
    gb.b_start(2)
    ga.a_finish()
    ga.b_start(3)
    pass_sums(0)
    ga.ready(0)
    start_sums(2)
    pass_sums(1)
    ga.b_finish(1)
    gb.b_finish(3)
    gb.b_forward(2)
    ga.b_forward(2)
    ga.ready(1)
    start_sums(3)
    pass_sums(2)
    ga.b_forward(3)
    gb.b_finish(2)
    ga.b_finish(2)
    gb.ready(2)
    gb.ready(3)
    start_sums(4)
    pass_sums(3)
    start_sums(5)
    ga.b_finish(3)
    pass_sums(4)
    ga.ready(2)
    start_sums(6)
    pass_sums(5)
    ga.ready(3)
    start_sums(7)
    pass_sums(6)
    end_sums(0)
    end_sums(1)
    pass_sums(7)
    for j in range(2, 8):
        end_sums(j)
    for copy in sends:
        copy.wait_send()


def fused(x, enc, wq, wk, wv, wo, mask, count):
    vmem = pltpu.VMEM
    return pl.pallas_call(
        kernel,
        out_shape=jax.ShapeDtypeStruct((128, 4096), BF16),
        in_specs=[pl.BlockSpec(memory_space=pl.ANY)] * 6
        + [pl.BlockSpec(memory_space=pltpu.VMEM)] * 2,
        out_specs=pl.BlockSpec(memory_space=pltpu.VMEM),
        scratch_shapes=[
            vmem((128, 4096), BF16),
            vmem((4, 128, 4096), BF16),
            vmem((4, 8, 256), F32),
            vmem((16, 16, 4096), BF16),
            vmem((4, 2, 2, 2, 512, 256), BF16),
            vmem((8, 512, 256), BF16),
            vmem((8, 512, 256), BF16),
            vmem((2, 4, 2, 2, 2, 256, 256), BF16),
            vmem((4, 2, 256, 256), BF16),
            vmem((2, 256, 256), F32),
            vmem((4, 256, 256), BF16),
            vmem((4, 256, 256), BF16),
            vmem((4, 512, 256), F32),
            vmem((4, 512, 256), BF16),
            vmem((4, 128, 1024), BF16),
            vmem((8, 4, 128, 512), F32),
            vmem((8, 2, 64, 512), BF16),
            vmem((8, 2, 64, 512), BF16),
            vmem((8, 2, 128, 512), BF16),
            vmem((8, 2, 128, 512), BF16),
            pltpu.SemaphoreType.DMA((MAX_COPIES,)),
            pltpu.SemaphoreType.DMA((MAX_COPIES,)),
            pltpu.SemaphoreType.DMA((8,)),
        ],
        compiler_params=pltpu.CompilerParams(
            collective_id=0, has_side_effects=True, vmem_limit_bytes=60 << 20
        ),
        name="cross_attention",
    )(x, enc, wq, wk, wv, wo, mask, count)


def shards(cand_states, enc_rows, w_query, w_key, w_value, w_out, tile_mask, counts):
    total = fused(
        cand_states[0, 0], enc_rows[0], w_query, w_key, w_value, w_out, tile_mask[0], counts[None]
    )
    return total[None, None]


def solution(mesh):
    return jax.shard_map(
        shards,
        mesh=mesh,
        in_specs=(
            P("prod", "cand", None, None),
            P("prod", "cand", None),
            P("prod", "cand"),
            P("prod", "cand"),
            P("prod", "cand"),
            P("cand", "prod"),
            P("prod", "cand", None),
            P("prod"),
        ),
        out_specs=P("prod", "cand", None, None),
        check_vma=False,
    )
```
